256 devices in a mesh: psg: 8 (over z), exp: 32 (over y, x, core).
Axes of the slice: x: 4, y: 4, z: 8, core: 2. Of those that a mesh axis runs over, the one named last changes fastest.
Arguments:
- hidden: bfloat16 [32, 8, 128, 2048], P('exp', 'psg')
- norm_gain: float32 [2048], replicated, may hold values from 0.5 to 2
- router: bfloat16 [2048, 32], replicated, may hold values from -0.125 to 0.125
- gate_proj: bfloat16 [32, 2048, 768], P('exp'), may hold values from -0.125 to 0.125
- up_proj: bfloat16 [32, 2048, 768], P('exp'), may hold values from -0.125 to 0.125
- down_proj: bfloat16 [32, 768, 2048], P('exp'), may hold values from -0.21875 to 0.21875
- final_gain: float32 [2048], replicated, may hold values from 0.5 to 2
- score_vector: bfloat16 [2048], replicated, may hold values from -0.125 to 0.125
- expert_ids: int32 [32, 8, 128, 8], P('exp', 'psg'), may hold values from 0 to 31, as said below
- grades: int32 [32, 8], P('exp'), may hold values from 0 to 4, as said below
- passage_ranks: int32 [32, 8], P('exp'), may hold values from 0 to 7, each once within a row
Outputs:
- loss: float32 [32], P('exp')
- scores: float32 [32, 8], P('exp', 'psg')
- grad_hidden: bfloat16 [32, 8, 128, 2048], P('exp', 'psg')
The draws below stay inside these ranges and needn't reach their ends.
Inputs may be any that keep to these rules, and one draw needn't show every extreme that they name: `expert_ids`: each token names 8 different experts. Among the tokens of one device each expert is named at most 36 times, and one expert, the same on every device, is named exactly 36 times on every device. `grades`: every query has some passage of grade 4. `passage_ranks`: each rank appears once in each query.
All inputs are finite; a program needn't handle non-finite values.
Results may differ from the reference program's by a relative error of at most 0.0067.
Values may be sent and summed in bfloat16 or wider, within the bound.
A program may use at most 128 MiB of HBM per device.

```python
import math
import jax
import jax.numpy as jnp
from jax import lax

D = 2048
FF = 768
TOP = 8
PSG_DEV = 1
PLEN = 128
TOK_DEV = 128
PASSAGES = 8
QUERIES = 32
EXPERTS = 32
CAP = 36


def draw_hidden(key, part):
    scale_key, channel_key, noise_key = jax.random.split(key, 3)
    token_scale = jnp.exp(jax.random.uniform(scale_key, (QUERIES, PASSAGES, PLEN, 1), jnp.float32, math.log(0.25), math.log(2.5)))
    channel_scale = jnp.exp(jax.random.uniform(channel_key, (1, 1, 1, D), jnp.float32, -0.5 * math.log(10.0), 0.5 * math.log(10.0)))
    noise = jax.random.normal(noise_key, (QUERIES, PASSAGES, PLEN, D), jnp.float32)
    return (noise * token_scale * channel_scale).astype(jnp.bfloat16)


def draw_grades(key, part):
    grade_key, best_key = jax.random.split(key)
    values = jax.random.randint(grade_key, (QUERIES, PASSAGES), 0, 5, jnp.int32)
    best_index = jax.random.randint(best_key, (QUERIES, 1), 0, PASSAGES, jnp.int32)
    return jnp.where(jnp.arange(PASSAGES, dtype=jnp.int32)[None, :] == best_index, 4, values).astype(jnp.int32)


def route_block(block_key, hot_expert, base_load, extra_load, spread_most):
    order_key, move_key, token_key, column_key = jax.random.split(block_key, 4)
    expert_range = jnp.arange(EXPERTS, dtype=jnp.int32)
    shuffled = jax.random.permutation(order_key, EXPERTS).astype(jnp.int32)
    priority = jnp.where(shuffled == hot_expert, -1, expert_range)
    ordering = shuffled[jnp.argsort(priority)]
    loads = jnp.where(expert_range == 0, CAP, base_load + (expert_range - 1 < extra_load).astype(jnp.int32))
    pair_count = min(8, (EXPERTS - 1) // 2)
    moves = jax.random.randint(move_key, (EXPERTS,), 0, spread_most + 1, jnp.int32)
    raise_mask = jnp.logical_and(expert_range >= 1, expert_range <= pair_count)
    moves_up = jnp.where(raise_mask, moves, 0)
    loads = loads + moves_up - jnp.roll(moves_up, pair_count)
    bounds = jnp.cumsum(loads)
    slot_index = jnp.arange(TOK_DEV * TOP, dtype=jnp.int32)
    label_rank = jnp.sum((bounds[None, :] <= slot_index[:, None]).astype(jnp.int32), axis=1)
    labels = ordering[label_rank].reshape(TOP, TOK_DEV).T
    token_order = jax.random.permutation(token_key, TOK_DEV)
    labels = labels[token_order]
    column_score = jax.random.randint(column_key, (TOK_DEV, TOP), 0, 1 << 20, jnp.int32) * TOP + jnp.arange(TOP, dtype=jnp.int32)[None, :]
    return jnp.take_along_axis(labels, jnp.argsort(column_score, axis=1), axis=1).astype(jnp.int32)


def draw_expert_ids(key, part):
    slot_total = TOK_DEV * TOP
    base_load = (slot_total - CAP) // (EXPERTS - 1)
    extra_load = (slot_total - CAP) % (EXPERTS - 1)
    spread_most = max(0, min(CAP - base_load - 1, base_load // 2))
    hot_key, block_key = jax.random.split(key)
    hot_expert = jax.random.randint(hot_key, (), 0, EXPERTS, jnp.int32)
    group_count = PASSAGES // PSG_DEV
    block_keys = jax.random.split(block_key, QUERIES * group_count)
    blocks = jax.vmap(lambda one_key: route_block(one_key, hot_expert, base_load, extra_load, spread_most))(block_keys)
    return blocks.reshape(QUERIES, PASSAGES, PLEN, TOP)


def shard_levels(own_key, shape, shards, smallest, top_value):
    loudness = 1.0
    for dim, parts in shards:
        steps = jax.random.uniform(jax.random.fold_in(jax.random.fold_in(own_key, 6), dim), (parts,), jnp.float32, smallest / len(shards), top_value / len(shards))
        loudness = loudness * jnp.repeat(jnp.exp(steps), shape[dim] // parts).reshape((-1,) + (1,) * (len(shape) - 1 - dim))
    return loudness


def centred(rng, dims, spread, reach, cuts=(), kind=jnp.bfloat16):
    factor_of = shard_levels(rng, dims, cuts, -0.22, 0.18) if cuts else 1.0
    drawn = jax.random.normal(rng, dims, jnp.float32) * spread * factor_of
    return jnp.minimum(jnp.maximum(drawn, -reach), reach).astype(kind)


def setup_inputs(seed: int = 0) -> dict:
    arg_keys = jax.random.split(jax.random.key(seed), 12)
    return {
        "hidden": draw_hidden(jax.random.fold_in(arg_keys[11], 71), 0),
        "norm_gain": jnp.clip(jnp.exp(jax.random.uniform(arg_keys[1], (D,), jnp.float32, math.log(0.5), math.log(2.0))), 0.5, 2.0),
        "router": centred(arg_keys[2], (D, EXPERTS), D ** -0.5, 0.125),
        "gate_proj": centred(arg_keys[3], (EXPERTS, D, FF), D ** -0.5, 0.125, ((0, 32),)),
        "up_proj": centred(arg_keys[4], (EXPERTS, D, FF), D ** -0.5, 0.125, ((0, 32),)),
        "down_proj": centred(arg_keys[5], (EXPERTS, FF, D), FF ** -0.5, 0.21875, ((0, 32),)),
        "final_gain": jnp.clip(jnp.exp(jax.random.uniform(arg_keys[6], (D,), jnp.float32, math.log(0.5), math.log(2.0))), 0.5, 2.0),
        "score_vector": centred(arg_keys[7], (D,), D ** -0.5, 0.125),
        "expert_ids": draw_expert_ids(jax.random.fold_in(arg_keys[11], 71), 0),
        "grades": draw_grades(jax.random.fold_in(arg_keys[11], 71), 0),
        "passage_ranks": jax.vmap(lambda own: jax.random.permutation(own, PASSAGES))(jax.random.split(arg_keys[10], QUERIES)).reshape((QUERIES, PASSAGES)).astype(jnp.int32),
    }


epsilon = 1e-06
loss_scale = 256.0
highest = lax.Precision.HIGHEST

def rms_scale(values):
    return lax.rsqrt(lax.optimization_barrier(jnp.mean(values * values, axis=-1, keepdims=True)) + epsilon)

def head_score(pooled, final_gain, score_vector):
    scaled = pooled * rms_scale(pooled) * final_gain
    return jnp.dot(scaled, score_vector.astype(jnp.float32), precision=highest)

def rank_loss(scores, grades, passage_ranks):
    grade_value = grades.astype(jnp.float32)
    worth_gain = jnp.exp2(grade_value)
    discount = 1.0 / jnp.log2(2.0 + passage_ranks.astype(jnp.float32))
    better_than = grades[None, :] > grades[:, None]
    equal_grade = grades[None, :] == grades[:, None]
    position = jnp.arange(grades.shape[0], dtype=jnp.int32)
    earlier = position[None, :] < position[:, None]
    ideal_rank = lax.optimization_barrier(jnp.sum(jnp.logical_or(better_than, jnp.logical_and(equal_grade, earlier)).astype(jnp.float32), axis=1))
    ideal_gain = jnp.sum((worth_gain - 1.0) / jnp.log2(2.0 + ideal_rank))
    ordered = (grades[:, None] > grades[None, :]).astype(jnp.float32)
    swap_gain = jnp.abs((worth_gain[:, None] - worth_gain[None, :]) * (discount[:, None] - discount[None, :])) / ideal_gain
    margin = scores[:, None] - scores[None, :]
    return jnp.sum(ordered * swap_gain * jax.nn.softplus(-margin))

def total_loss(scores, grades, passage_ranks):
    every = jax.vmap(rank_loss)(scores, grades, passage_ranks)
    return (jnp.sum(every), every)

def pick_gates(normed, router, picked_ids):
    expert_total = router.shape[1]
    logits = jnp.dot(normed, router, preferred_element_type=jnp.float32)
    onehot = (picked_ids[:, :, None] == jnp.arange(expert_total, dtype=jnp.int32)[None, None, :]).astype(jnp.float32)
    chosen = jnp.einsum('nke,ne->nk', onehot, logits, precision=highest)
    weights = jnp.exp(chosen)
    return (weights / lax.optimization_barrier(jnp.sum(weights, axis=1, keepdims=True)), onehot)

def gate_parts(pre_gate):
    sigmoid_gate = jax.nn.sigmoid(pre_gate)
    return (pre_gate * sigmoid_gate, sigmoid_gate * (1.0 + pre_gate * (1.0 - sigmoid_gate)))

def norm_back(flat_rows, inverse, norm_gain, d_normed):
    scaled = d_normed * norm_gain
    return inverse * scaled - flat_rows * inverse * inverse * inverse * lax.optimization_barrier(jnp.mean(flat_rows * scaled, axis=-1, keepdims=True))

def to_low(values):
    return lax.optimization_barrier(values.astype(jnp.bfloat16)).astype(jnp.float32)

def reference(hidden, norm_gain, router, gate_proj, up_proj, down_proj, final_gain, score_vector, expert_ids, grades, passage_ranks):
    passage_total = QUERIES * PASSAGES
    token_count = passage_total * PLEN
    slot_count = token_count * TOP
    row_limit = CAP * (token_count // TOK_DEV)
    flat_rows = hidden.reshape(token_count, D).astype(jnp.float32)
    inverse = rms_scale(flat_rows)
    normed = (flat_rows * inverse * norm_gain).astype(jnp.bfloat16)
    picked_ids = expert_ids.reshape(token_count, TOP)
    gate_values, onehot = pick_gates(normed, router, picked_ids)
    gate_low = to_low(gate_values).reshape(slot_count)
    slot_ids = picked_ids.reshape(slot_count)
    slot_hits = onehot.reshape(slot_count, EXPERTS).astype(jnp.int32)
    slot_rank = lax.optimization_barrier(jnp.sum((jnp.cumsum(slot_hits, axis=0) - slot_hits) * slot_hits, axis=1))
    table = jnp.full((EXPERTS, row_limit), slot_count, jnp.int32)
    table = table.at[slot_ids, slot_rank].set(jnp.arange(slot_count, dtype=jnp.int32))
    passage_ids = jnp.arange(passage_total, dtype=jnp.int32)

    def expert_rows(slot_row):
        valid = slot_row < slot_count
        safe_slot = jnp.where(valid, slot_row, 0)
        token_row = safe_slot // TOP
        weight = jnp.where(valid, gate_low[safe_slot], 0.0)
        belongs = (token_row[:, None] // PLEN == passage_ids[None, :]).astype(jnp.float32)
        return (token_row, weight, belongs)

    def expert_front(gate_one, up_one, token_row):
        inputs = normed[token_row].astype(jnp.float32)
        pre_gate = jnp.dot(inputs, gate_one.astype(jnp.float32), precision=highest)
        pre_up = jnp.dot(inputs, up_one.astype(jnp.float32), precision=highest)
        silu_gate, slope = gate_parts(pre_gate)
        act_low = to_low(silu_gate * pre_up)
        return (pre_up, silu_gate, slope, act_low)

    def forward_one(operands):
        gate_one, up_one, down_one, slot_row = operands
        token_row, weight, belongs = expert_rows(slot_row)
        unused_up, silu_gate, slope, act_low = expert_front(gate_one, up_one, token_row)
        passage_part = jnp.dot((belongs * weight[:, None]).T, act_low, precision=highest)
        return jnp.dot(passage_part, down_one.astype(jnp.float32), precision=highest)
    moe_terms = lax.map(forward_one, (gate_proj, up_proj, down_proj, table))
    pooled = (lax.optimization_barrier(jnp.sum(flat_rows.reshape(passage_total, PLEN, D), axis=1)) + lax.optimization_barrier(jnp.sum(moe_terms, axis=0))) / PLEN
    scores = head_score(pooled, final_gain, score_vector).reshape(QUERIES, PASSAGES)
    (unused_total, losses), loss_grad = jax.value_and_grad(total_loss, has_aux=True)(scores, grades, passage_ranks)
    unused_score, head_back = jax.vjp(lambda values: head_score(values, final_gain, score_vector), pooled)
    d_vector = head_back(loss_grad.reshape(passage_total) * loss_scale)[0] / PLEN

    def backward_one(carry, operands):
        d_normed, slot_grad = carry
        gate_one, up_one, down_one, slot_row = operands
        token_row, weight, belongs = expert_rows(slot_row)
        pre_up, silu_gate, slope, act_low = expert_front(gate_one, up_one, token_row)
        near_table = jnp.dot(d_vector, down_one.astype(jnp.float32).T, precision=highest)
        near_rows = jnp.dot(belongs, near_table, precision=highest)
        d_act = weight[:, None] * near_rows
        d_gate = to_low(d_act * pre_up * slope)
        d_up = to_low(d_act * silu_gate)
        pick_grad = jnp.dot(d_gate, gate_one.astype(jnp.float32).T, precision=highest) + jnp.dot(d_up, up_one.astype(jnp.float32).T, precision=highest)
        pick_grad = to_low(pick_grad)
        gate_grad = to_low(lax.optimization_barrier(jnp.sum(act_low * near_rows, axis=1)))
        valid = slot_row < slot_count
        d_normed = d_normed.at[token_row].add(jnp.where(valid[:, None], pick_grad, 0.0))
        slot_grad = slot_grad.at[slot_row].set(gate_grad, mode='drop')
        return ((d_normed, slot_grad), None)
    start = (jnp.zeros((token_count, D), jnp.float32), jnp.zeros((slot_count,), jnp.float32))
    (d_normed, slot_grad), unused_rest = lax.scan(backward_one, start, (gate_proj, up_proj, down_proj, table))
    slot_gate = slot_grad.reshape(token_count, TOP)
    d_logit = gate_values * (slot_gate - lax.optimization_barrier(jnp.sum(gate_values * slot_gate, axis=1, keepdims=True)))
    dense_logit = jnp.einsum('nk,nke->ne', d_logit, onehot, precision=highest)
    d_normed = d_normed + jnp.dot(dense_logit, router.astype(jnp.float32).T, precision=highest)
    grad_flat = norm_back(flat_rows, inverse, norm_gain, d_normed)
    grad_hidden = grad_flat.reshape(passage_total, PLEN, D) + d_vector[:, None, :]
    return (losses, scores, grad_hidden.reshape(QUERIES, PASSAGES, PLEN, D).astype(jnp.bfloat16))
```

```python
import jax
import jax.numpy as jnp
from jax import lax
from jax.experimental import pallas as pl
from jax.experimental.pallas import tpu as pltpu
from jax.sharding import PartitionSpec as P

MESH = pl.DeviceIdType.MESH
EPS = 1e-06
LOSS_SCALE = 256.0
SLOTS = 40
MARK = 36
WAYS = 32
NN = (((1,), (0,)), ((), ()))
NT = (((1,), (1,)), ((), ()))
TN = (((0,), (0,)), ((), ()))

GROUPS = (
    ((0, 0), (1, 0)),
    ((3, 0), (0, 1)),
    ((0, 3), (1, 1)),
    ((1, 3), (3, 1)),
    ((3, 3), (2, 0)),
    ((0, 2), (2, 1)),
    ((2, 3), (1, 2)),
    ((3, 2), (2, 2)),
)


def dot(a, b, dims):
    return lax.dot_general(a, b, dims, preferred_element_type=jnp.float32)


def split3(v):
    hi = v.astype(jnp.bfloat16).astype(jnp.float32)
    rest = v - hi
    mid = rest.astype(jnp.bfloat16).astype(jnp.float32)
    low = rest - mid
    return jnp.concatenate([hi, mid, low], axis=0).astype(jnp.bfloat16)


def kernel(
    hid, ids_t, gain, rout_t, fgain, svec, grades, ranks, wg_hbm, wu_hbm, wd_hbm,
    loss_o, score_o, out_o,
    xbuf, wg, wu, wd, gate_s, rinv, toks, gsend, grecv, own_rank, rk,
    xg, aref, bref, actr, ppart, tsend, trecv, hbuf, h3, nref, zbuf,
    rs, rrecv, gown, acc,
    wsem, ag_s, ag_r, pt_s, pt_r, small_s, small_r, ret_s, ret_r,
):
    tokens, width = hid.shape
    units = wg.shape[1]
    half, quarter = tokens // 2, tokens // 4
    planes = zbuf.shape[0]
    me = lax.axis_index("exp")
    z = lax.axis_index("psg")
    core = lax.rem(me, 2)
    cx = lax.rem(lax.div(me, 2), 4)
    cy = lax.div(me, 8)

    def at(dx, dy, other=0):
        side = (1 - core) if other else core
        return (lax.rem(cy + dy, 4) * 4 + lax.rem(cx + dx, 4)) * 2 + side

    barrier = pltpu.get_barrier_semaphore()

    def greet(i, carry):
        pl.semaphore_signal(
            barrier, inc=1, device_id={"exp": lax.rem(me + i, WAYS)}, device_id_type=MESH
        )
        return carry

    lax.fori_loop(1, WAYS, greet, 0)
    for i in range(1, planes):
        pl.semaphore_signal(
            barrier, inc=1, device_id={"psg": lax.rem(z + i, planes)}, device_id_type=MESH
        )
    loads = [
        pltpu.make_async_copy(wg_hbm, wg, wsem.at[0]),
        pltpu.make_async_copy(wu_hbm, wu, wsem.at[1]),
        pltpu.make_async_copy(wd_hbm, wd, wsem.at[2]),
    ]
    for load in loads:
        load.start()

    toks[...] = jnp.zeros_like(toks)

    def norm_rows(i, carry):
        rows = pl.ds(pl.multiple_of(i * 16, 16), 16)
        h = hid[rows, :].astype(jnp.float32)
        r = lax.rsqrt(jnp.mean(h * h, axis=1, keepdims=True) + EPS)
        rinv[rows, :] = r
        toks[...] += jnp.sum(h, axis=0, keepdims=True)
        xbuf[me, rows, :] = (h * r * gain[...]).astype(jnp.bfloat16)
        return carry

    lax.fori_loop(0, tokens // 16, norm_rows, 0)
    pl.semaphore_wait(barrier, WAYS - 1 + planes - 1)

    pending = []

    def offset(h, du, dv):
        du, dv = du % 4, dv % 4
        return (du, dv) if h == 0 else (dv, du)

    def spot(h, du, dv):
        ox, oy = offset(h, du, dv)
        return oy * 4 + ox

    def rows_of(h, q):
        start = h * half
        if q is None:
            return pl.ds(start, half)
        return pl.ds(start + q * quarter, quarter)

    def send(h, du, dv, q, su, sv):
        block = at(*offset(h, du, dv))
        piece = xbuf.at[block, rows_of(h, q)]
        k = len([1 for kind, _ in pending if kind == 0])
        copy = pltpu.make_async_remote_copy(
            src_ref=piece,
            dst_ref=piece,
            send_sem=ag_s.at[k],
            recv_sem=ag_r.at[h, spot(h, du - su, dv - sv), q or 0],
            device_id={"exp": at(*offset(h, su, sv))},
            device_id_type=MESH,
        )
        copy.start()
        pending.append((0, copy))

    def share(h, du, dv):
        block = at(*offset(h, du, dv))
        piece = xbuf.at[block, rows_of(h, None)]
        k = spot(h, du, dv)
        copy = pltpu.make_async_remote_copy(
            src_ref=piece,
            dst_ref=piece,
            send_sem=pt_s.at[h, k],
            recv_sem=pt_r.at[h, k],
            device_id={"exp": at(0, 0, 1)},
            device_id_type=MESH,
        )
        copy.start()
        pending.append((1, copy))

    def arrive(h, du, dv, q):
        block = at(*offset(h, du, dv))
        piece = xbuf.at[block, rows_of(h, q)]
        pltpu.make_async_copy(piece, piece, ag_r.at[h, spot(h, du, dv), q or 0]).wait()

    for h in (0, 1):
        send(h, 0, 0, None, 1, 0)
        send(h, 0, 0, None, 3, 0)
    for h in (0, 1):
        send(h, 0, 0, None, 0, 1)
        send(h, 0, 0, None, 0, 3)
    for h in (0, 1):
        share(h, 0, 0)

    logits = dot(rout_t[...], xbuf[me], NT)
    experts = lax.broadcasted_iota(jnp.int32, (WAYS, tokens), 0)
    picked = ids_t[0:1, :] == experts
    for k in range(1, ids_t.shape[0]):
        picked = jnp.logical_or(picked, ids_t[k : k + 1, :] == experts)
    weights = jnp.where(picked, jnp.exp(logits), 0.0)
    gates = weights / jnp.sum(weights, axis=0, keepdims=True)
    gate_s[...] = gates
    gate_low = gates.astype(jnp.bfloat16).astype(jnp.float32)
    gsend[:, 0, :] = jnp.where(picked, gate_low, -1.0)
    before = (
        lax.broadcasted_iota(jnp.int32, (tokens, tokens), 0)
        < lax.broadcasted_iota(jnp.int32, (tokens, tokens), 1)
    ).astype(jnp.float32).astype(jnp.bfloat16)

    def rank_of(mask):
        place = dot(mask.astype(jnp.float32).astype(jnp.bfloat16), before, NN)
        return jnp.where(mask, place, -1.0)

    own_rank[:, 0, :] = rank_of(picked)

    def to_all(source, target, which):
        def one(i, carry):
            e = lax.rem(me + i, WAYS)
            pltpu.make_async_remote_copy(
                src_ref=source(e),
                dst_ref=target.at[me],
                send_sem=small_s.at[which],
                recv_sem=small_r.at[which],
                device_id={"exp": e},
                device_id_type=MESH,
            ).start()
            return carry

        lax.fori_loop(1, WAYS, one, 0)

    def from_all(target, which, count=WAYS - 1):
        block = target.at[pl.ds(0, count)]
        pltpu.make_async_copy(block, block, small_r.at[which]).wait()

    def sent_all(target, which, count=WAYS - 1):
        block = target.at[pl.ds(0, count)]
        pltpu.make_async_copy(block, block, small_s.at[which]).wait()

    to_all(lambda e: gsend.at[e], grecv, 0)
    grecv[me] = gsend[me]

    for h in (0, 1):
        arrive(h, 3, 0, None)
        send(h, 3, 0, 0, 1, 0)
        send(h, 3, 0, None, 0, 1)
        send(h, 3, 0, None, 0, 3)
        arrive(h, 1, 0, None)
        send(h, 1, 0, 1, 3, 0)
        send(h, 1, 0, None, 0, 1)
        send(h, 1, 0, None, 0, 3)
    for h in (0, 1):
        arrive(h, 0, 3, None)
        send(h, 0, 3, 0, 0, 1)
        arrive(h, 0, 1, None)
        send(h, 0, 1, 1, 0, 3)
    for h in (0, 1):
        for du, dv in ((3, 0), (1, 0), (0, 3), (0, 1)):
            share(h, du, dv)

    from_all(grecv, 0)
    everyone = grecv[:, 0, :]
    rk[:, 0, :] = rank_of(everyone >= 0.0)
    for load in loads[:2]:
        load.wait()
    slot = lax.broadcasted_iota(jnp.int32, (SLOTS, tokens), 0).astype(jnp.float32)
    row_id = lax.broadcasted_iota(jnp.int32, (SLOTS, tokens), 0)

    def sources(group, sign=1):
        return [(at((sign * dx) % 4, (sign * dy) % 4, o), dx, dy, o) for dx, dy in group for o in (0, 1)]

    def forward(group):
        for dx, dy in group:
            for h in (0, 1):
                block = at(dx, dy, 1)
                piece = xbuf.at[block, rows_of(h, None)]
                pltpu.make_async_copy(piece, piece, pt_r.at[h, dy * 4 + dx]).wait()
        members = [s for s, _, _, _ in sources(group)]
        rows, gate_col = [], []
        for s in members:
            hit = slot == rk[s]
            one = jnp.where(hit, 1.0, 0.0)
            rows.append(dot(one.astype(jnp.bfloat16), xbuf[s], NN))
            gate_col.append(jnp.sum(jnp.where(hit, grecv[s], 0.0), axis=1, keepdims=True))
        xg[...] = jnp.concatenate(rows, axis=0).astype(jnp.bfloat16)
        weight = jnp.concatenate(gate_col, axis=0)
        step = min(256, units)

        def tile(n, carry):
            cols = pl.ds(pl.multiple_of(n * step, step), step)
            pre_gate = dot(xg[...], wg[:, cols], NN)
            pre_up = dot(xg[...], wu[:, cols], NN)
            sig = 1.0 / (1.0 + jnp.exp(-pre_gate))
            silu = pre_gate * sig
            slope = sig * (1.0 + pre_gate * (1.0 - sig))
            act = (silu * pre_up).astype(jnp.bfloat16).astype(jnp.float32)
            to_gate = weight * (pre_up * slope)
            to_up = weight * silu
            part = weight * act
            for i, s in enumerate(members):
                span = slice(i * SLOTS, (i + 1) * SLOTS)
                aref[s, :, cols] = to_gate[span]
                bref[s, :, cols] = to_up[span]
                actr[s, :, cols] = act[span]
                ppart[s, :, cols] = jnp.sum(part[span], axis=0, keepdims=True)
            return carry

        lax.fori_loop(0, units // step, tile, 0)

    forward(GROUPS[0])
    for h in (0, 1):
        for q in (0, 1):
            arrive(h, 2, 0, q)
            send(h, 2, 0, q, 0, 1)
            send(h, 2, 0, q, 0, 3)
        share(h, 2, 0)
    forward(GROUPS[1])
    for h in (0, 1):
        for du in (3, 1):
            arrive(h, du, 3, None)
            send(h, du, 3, 0, 0, 1)
            arrive(h, du, 1, None)
            send(h, du, 1, 1, 0, 3)
            share(h, du, 3)
            share(h, du, 1)
    forward(GROUPS[2])
    for h in (0, 1):
        arrive(h, 2, 3, 0)
        send(h, 2, 3, 0, 0, 1)
        arrive(h, 2, 1, 1)
        send(h, 2, 1, 1, 0, 3)
        arrive(h, 2, 3, 1)
        arrive(h, 2, 1, 0)
        share(h, 2, 3)
        share(h, 2, 1)
    forward(GROUPS[3])
    for h in (0, 1):
        arrive(h, 0, 2, 0)
        arrive(h, 0, 2, 1)
        share(h, 0, 2)
    forward(GROUPS[4])
    for h in (0, 1):
        for du in (3, 1):
            arrive(h, du, 2, 0)
            arrive(h, du, 2, 1)
            share(h, du, 2)
    forward(GROUPS[5])
    for h in (0, 1):
        arrive(h, 2, 2, 0)
        arrive(h, 2, 2, 1)
        share(h, 2, 2)
    forward(GROUPS[6])
    forward(GROUPS[7])

    loads[2].wait()
    xg[0 : 3 * WAYS, 0:units] = split3(ppart[:, 0, :])
    wide = min(256, width)

    def term_tile(n, carry):
        cols = pl.ds(pl.multiple_of(n * wide, wide), wide)
        t = dot(xg[0 : 3 * WAYS, 0:units], wd[:, cols], NN)
        tsend[:, 0, cols] = t[0:WAYS] + (t[WAYS : 2 * WAYS] + t[2 * WAYS : 3 * WAYS])
        return carry

    lax.fori_loop(0, width // wide, term_tile, 0)
    to_all(lambda e: tsend.at[e], trecv, 1)
    trecv[me] = tsend[me]
    from_all(trecv, 1)
    pooled = (toks[...] + jnp.sum(trecv[...], axis=0)) / tokens
    inv = lax.rsqrt(jnp.mean(pooled * pooled, axis=1, keepdims=True) + EPS)
    head_dir = fgain[...] * svec[...].astype(jnp.float32)
    score = jnp.sum(pooled * inv * head_dir, axis=1, keepdims=True)
    lean = jnp.mean(pooled * head_dir, axis=1, keepdims=True)
    head = inv * head_dir - pooled * (inv * inv * inv * lean)
    hbuf[me] = head
    zbuf[z] = jnp.broadcast_to(score, (1, zbuf.shape[2]))
    to_all(lambda e: hbuf.at[me], hbuf, 2)
    for i in range(1, planes):
        pltpu.make_async_remote_copy(
            src_ref=zbuf.at[z],
            dst_ref=zbuf.at[z],
            send_sem=small_s.at[3],
            recv_sem=small_r.at[3],
            device_id={"psg": lax.rem(z + i, planes)},
            device_id_type=MESH,
        ).start()
    from_all(hbuf, 2)
    h3[...] = split3(hbuf[:, 0, :])
    step = min(256, units)

    def near_tile(n, carry):
        cols = pl.ds(pl.multiple_of(n * step, step), step)
        t = dot(h3[...], wd[cols, :], NT)
        nref[:, 0, cols] = t[0:WAYS] + (t[WAYS : 2 * WAYS] + t[2 * WAYS : 3 * WAYS])
        return carry

    lax.fori_loop(0, units // step, near_tile, 0)

    back = []

    def backward(group):
        members = sources(group)
        gates_in, ups_in = [], []
        for s, _, _, _ in members:
            near = nref[s]
            gates_in.append(aref[s] * near)
            ups_in.append(bref[s] * near)
        d_gate = jnp.concatenate(gates_in, axis=0).astype(jnp.bfloat16)
        d_up = jnp.concatenate(ups_in, axis=0).astype(jnp.bfloat16)
        xg[:, 0:units] = d_gate
        xg[:, units : 2 * units] = d_up

        def tile(n, carry):
            cols = pl.ds(pl.multiple_of(n * wide, wide), wide)
            g = dot(xg[:, 0:units], wg[cols, :], NT)
            g = g + dot(xg[:, units : 2 * units], wu[cols, :], NT)
            for i, (s, _, _, _) in enumerate(members):
                rs[s, :, cols] = g[i * SLOTS : (i + 1) * SLOTS].astype(jnp.bfloat16)
            return carry

        lax.fori_loop(0, width // wide, tile, 0)
        for s, dx, dy, o in members:
            gg = jnp.sum(actr[s] * nref[s], axis=1, keepdims=True)
            dense = jnp.sum(jnp.where(slot == rk[s], gg, 0.0), axis=0, keepdims=True)
            first = rs[s, :, 0:tokens].astype(jnp.float32)
            rs[s, :, 0:tokens] = jnp.where(row_id == MARK, dense, first).astype(jnp.bfloat16)
        for s, dx, dy, o in members:
            if (dx, dy, o) == (0, 0, 0):
                continue
            k = (dy * 4 + dx) * 2 + o
            mirror = (((-dy) % 4) * 4 + (-dx) % 4) * 2 + o
            copy = pltpu.make_async_remote_copy(
                src_ref=rs.at[s],
                dst_ref=rrecv.at[me],
                send_sem=ret_s.at[k],
                recv_sem=ret_r.at[mirror],
                device_id={"exp": s},
                device_id_type=MESH,
            )
            copy.start()
            back.append(copy)

    for group in reversed(GROUPS):
        backward(group)

    from_all(zbuf, 3, planes - 1)
    eye_r = lax.broadcasted_iota(jnp.int32, (planes, planes), 0)
    eye_c = lax.broadcasted_iota(jnp.int32, (planes, planes), 1)
    eye = eye_r == eye_c

    def column(row):
        return jnp.sum(jnp.where(eye, row, 0.0), axis=1, keepdims=True)

    g_row = grades[...].astype(jnp.float32)
    g_col = column(g_row)
    s_col = zbuf[:, 0, 0:1]
    s_row = jnp.sum(jnp.where(eye, s_col, 0.0), axis=0, keepdims=True)
    ln2 = 0.6931471805599453
    d_row = ln2 / jnp.log(2.0 + ranks[...].astype(jnp.float32))
    d_col = column(d_row)
    worth_row = jnp.exp2(g_row)
    worth_col = column(worth_row)
    ahead = jnp.logical_or(g_row > g_col, jnp.logical_and(g_row == g_col, eye_c < eye_r))
    ideal = jnp.sum(jnp.where(ahead, 1.0, 0.0), axis=1, keepdims=True)
    ideal_gain = jnp.sum((worth_col - 1.0) * ln2 / jnp.log(2.0 + ideal), axis=0, keepdims=True)
    swap = jnp.abs((worth_col - worth_row) * (d_col - d_row)) / ideal_gain
    swap = jnp.where(g_col > g_row, swap, 0.0)
    margin = s_col - s_row
    soft = jnp.maximum(-margin, 0.0) + jnp.log(1.0 + jnp.exp(-jnp.abs(margin)))
    loss_o[0] = jnp.sum(swap * soft)
    pull = swap / (1.0 + jnp.exp(margin))
    d_own = jnp.sum(jnp.where(eye_c == z, pull, 0.0) - jnp.where(eye_r == z, pull, 0.0))
    score_o[0, 0] = jnp.sum(score)
    scale = d_own * (LOSS_SCALE / tokens)

    acc[...] = jnp.zeros_like(acc)
    for group in reversed(GROUPS):
        members = sources(group, -1)
        hits = []
        for e, dx, dy, o in members:
            mx, my = (-dx) % 4, (-dy) % 4
            if (dx, dy, o) == (0, 0, 0):
                rrecv[e] = rs[e]
            else:
                block = rrecv.at[e]
                pltpu.make_async_copy(block, block, ret_r.at[(my * 4 + mx) * 2 + o]).wait()
            hits.append(jnp.where(slot == own_rank[e], 1.0, 0.0))
            mark = rrecv[e, :, 0:tokens].astype(jnp.float32)
            gown[e] = jnp.sum(jnp.where(row_id == MARK, mark, 0.0), axis=0, keepdims=True)
        hit = jnp.concatenate(hits, axis=0).astype(jnp.bfloat16)

        def tile(n, carry):
            cols = pl.ds(pl.multiple_of(n * wide, wide), wide)
            rows = jnp.concatenate(
                [rrecv[e, :, cols].astype(jnp.float32) for e, _, _, _ in members], axis=0
            ).astype(jnp.bfloat16)
            acc[:, cols] += dot(hit, rows, TN)
            return carry

        lax.fori_loop(0, width // wide, tile, 0)

    gate_grad = gown[:, 0, :]
    gates = gate_s[...]
    d_logit = gates * (gate_grad - jnp.sum(gates * gate_grad, axis=0, keepdims=True))
    d_logit = split3(d_logit)
    rout3 = jnp.concatenate([rout_t[...]] * 3, axis=0)
    acc[...] += dot(d_logit, rout3, TN)
    head = hbuf[me]

    def finish(i, carry):
        rows = pl.ds(pl.multiple_of(i * 16, 16), 16)
        h = hid[rows, :].astype(jnp.float32)
        r = rinv[rows, :]
        scaled = acc[rows, :] * gain[...]
        lean = jnp.mean(h * scaled, axis=1, keepdims=True)
        full = r * scaled - h * (r * r * r * lean) + head
        out_o[rows, :] = (full * scale).astype(jnp.bfloat16)
        return carry

    lax.fori_loop(0, tokens // 16, finish, 0)
    for _, copy in pending:
        copy.wait_send()
    for copy in back:
        copy.wait_send()
    sent_all(gsend, 0)
    sent_all(tsend, 1)
    sent_all(hbuf, 2)
    sent_all(zbuf, 3, planes - 1)


def local(
    hidden,
    norm_gain,
    router,
    gate_proj,
    up_proj,
    down_proj,
    final_gain,
    score_vector,
    expert_ids,
    grades,
    passage_ranks,
):
    tokens, width = hidden.shape[2:]
    units = gate_proj.shape[2]
    planes = lax.axis_size("psg")
    f32, bf16 = jnp.float32, jnp.bfloat16
    vmem = pl.BlockSpec(memory_space=pltpu.VMEM)
    any_space = pl.BlockSpec(memory_space=pl.ANY)
    smem = pl.BlockSpec(memory_space=pltpu.SMEM)
    scratch = [
        pltpu.VMEM((WAYS, tokens, width), bf16),
        pltpu.VMEM((width, units), bf16),
        pltpu.VMEM((width, units), bf16),
        pltpu.VMEM((units, width), bf16),
        pltpu.VMEM((WAYS, tokens), f32),
        pltpu.VMEM((tokens, 1), f32),
        pltpu.VMEM((1, width), f32),
        pltpu.VMEM((WAYS, 1, tokens), f32),
        pltpu.VMEM((WAYS, 1, tokens), f32),
        pltpu.VMEM((WAYS, 1, tokens), f32),
        pltpu.VMEM((WAYS, 1, tokens), f32),
        pltpu.VMEM((4 * SLOTS, max(width, 2 * units)), bf16),
        pltpu.VMEM((WAYS, SLOTS, units), f32),
        pltpu.VMEM((WAYS, SLOTS, units), f32),
        pltpu.VMEM((WAYS, SLOTS, units), f32),
        pltpu.VMEM((WAYS, 1, units), f32),
        pltpu.VMEM((WAYS, 1, width), f32),
        pltpu.VMEM((WAYS, 1, width), f32),
        pltpu.VMEM((WAYS, 1, width), f32),
        pltpu.VMEM((3 * WAYS, width), bf16),
        pltpu.VMEM((WAYS, 1, units), f32),
        pltpu.VMEM((planes, 1, tokens), f32),
        pltpu.VMEM((WAYS, SLOTS, width), bf16),
        pltpu.VMEM((WAYS, SLOTS, width), bf16),
        pltpu.VMEM((WAYS, 1, tokens), f32),
        pltpu.VMEM((tokens, width), f32),
        pltpu.SemaphoreType.DMA((3,)),
        pltpu.SemaphoreType.DMA((44,)),
        pltpu.SemaphoreType.DMA((2, 16, 2)),
        pltpu.SemaphoreType.DMA((2, 16)),
        pltpu.SemaphoreType.DMA((2, 16)),
        pltpu.SemaphoreType.DMA((4,)),
        pltpu.SemaphoreType.DMA((4,)),
        pltpu.SemaphoreType.DMA((WAYS,)),
        pltpu.SemaphoreType.DMA((WAYS,)),
    ]
    loss, score, grad = pl.pallas_call(
        kernel,
        out_shape=(
            jax.ShapeDtypeStruct((1,), f32),
            jax.ShapeDtypeStruct((1, 1), f32),
            jax.ShapeDtypeStruct((tokens, width), bf16),
        ),
        in_specs=[vmem] * 8 + [any_space] * 3,
        out_specs=(smem, smem, vmem),
        scratch_shapes=scratch,
        compiler_params=pltpu.CompilerParams(
            collective_id=0, has_side_effects=True, vmem_limit_bytes=62 * 1024 * 1024
        ),
        name="expert_block",
    )(
        hidden.reshape(tokens, width),
        expert_ids.reshape(tokens, -1).T,
        norm_gain.reshape(1, width),
        router.T,
        final_gain.reshape(1, width),
        score_vector.reshape(1, width),
        grades,
        passage_ranks,
        gate_proj[0],
        up_proj[0],
        down_proj[0],
    )
    return loss, score, grad.reshape(1, 1, tokens, width)


def solution(mesh):
    placed = (
        P("exp", "psg", None, None),
        P(),
        P(),
        P("exp", None, None),
        P("exp", None, None),
        P("exp", None, None),
        P(),
        P(),
        P("exp", "psg", None, None),
        P("exp", None),
        P("exp", None),
    )
    return jax.shard_map(
        local,
        mesh=mesh,
        in_specs=placed,
        out_specs=(P("exp"), P("exp", "psg"), P("exp", "psg", None, None)),
        check_vma=False,
    )
```

```python
import jax
import jax.numpy as jnp
from jax import lax
from jax.experimental import pallas as pl
from jax.experimental.pallas import tpu as pltpu
from jax.sharding import PartitionSpec as P

MESH = pl.DeviceIdType.MESH
EPS = 1e-06
LOSS_SCALE = 256.0
SLOTS = 40
WAYS = 32
NN = (((1,), (0,)), ((), ()))
NT = (((1,), (1,)), ((), ()))
TN = (((0,), (0,)), ((), ()))

GROUPS = (
    ((0, 0), (1, 0)),
    ((3, 0), (0, 1)),
    ((0, 3), (1, 1)),
    ((1, 3), (3, 1)),
    ((3, 3), (2, 0)),
    ((0, 2), (2, 1)),
    ((2, 3), (1, 2)),
    ((3, 2), (2, 2)),
)

BACK_GROUPS = (
    ((2, 2), (1, 2)),
    ((2, 1), (3, 2)),
    ((2, 3), (2, 0)),
    ((0, 2), (1, 1)),
    ((1, 3), (3, 1)),
    ((3, 3), (1, 0)),
    ((0, 1), (3, 0)),
    ((0, 3), (0, 0)),
)
RELAYS = (
    ((0, 2, 2), (1, 2, 2), (0, 1, 2)),
    ((1, 2, 1), (0, 2, 1), (1, 1, 2), (0, 3, 2), (1, 2, 3)),
    ((0, 2, 3), (1, 3, 2), (1, 0, 2)),
    ((0, 0, 2), (0, 1, 1), (1, 1, 1), (1, 2, 0), (0, 2, 0)),
    ((0, 1, 3), (1, 3, 1), (0, 3, 1), (1, 1, 3)),
    ((0, 3, 3), (1, 3, 3), (0, 1, 0), (1, 0, 1)),
    ((0, 0, 1), (1, 1, 0), (0, 3, 0), (1, 0, 3)),
    ((0, 0, 3), (1, 3, 0), (0, 0, 0), (1, 0, 0)),
)


def dot(a, b, dims):
    return lax.dot_general(a, b, dims, preferred_element_type=jnp.float32)


def split3(v):
    hi = v.astype(jnp.bfloat16).astype(jnp.float32)
    rest = v - hi
    mid = rest.astype(jnp.bfloat16).astype(jnp.float32)
    low = rest - mid
    return jnp.concatenate([hi, mid, low], axis=0).astype(jnp.bfloat16)


def kernel(
    hid, ids_t, gain, rout_t, fgain, svec, grades, ranks, wg_hbm, wu_hbm, wd_hbm,
    loss_o, score_o, out_o,
    xbuf, wg, wu, wd, gate_s, rinv, toks, gsend, grecv, rk,
    xg, aref, bref, actr, ppart, tsend, trecv, hbuf, h3, nref, zbuf,
    psend, precv, vq, vf, uq, uf, ggsend, gown, acc,
    wsem, ag_s, ag_r, pt_s, pt_r, small_s, small_r, pr_s, pr_r, tr_s, vq_r, vf_r, uq_r, uf_r,
):
    tokens, width = hid.shape
    units = wg.shape[1]
    half, quarter = tokens // 2, tokens // 4
    planes = zbuf.shape[0]
    me = lax.axis_index("exp")
    z = lax.axis_index("psg")
    core = lax.rem(me, 2)
    cx = lax.rem(lax.div(me, 2), 4)
    cy = lax.div(me, 8)

    def at(dx, dy, other=0):
        side = (1 - core) if other else core
        return (lax.rem(cy + dy, 4) * 4 + lax.rem(cx + dx, 4)) * 2 + side

    barrier = pltpu.get_barrier_semaphore()

    def greet(i, carry):
        pl.semaphore_signal(
            barrier, inc=1, device_id={"exp": lax.rem(me + i, WAYS)}, device_id_type=MESH
        )
        return carry

    lax.fori_loop(1, WAYS, greet, 0)
    for i in range(1, planes):
        pl.semaphore_signal(
            barrier, inc=1, device_id={"psg": lax.rem(z + i, planes)}, device_id_type=MESH
        )
    loads = [
        pltpu.make_async_copy(wg_hbm, wg, wsem.at[0]),
        pltpu.make_async_copy(wu_hbm, wu, wsem.at[1]),
        pltpu.make_async_copy(wd_hbm, wd, wsem.at[2]),
    ]
    for load in loads:
        load.start()

    toks[...] = jnp.zeros_like(toks)

    def norm_rows(i, carry):
        rows = pl.ds(pl.multiple_of(i * 16, 16), 16)
        h = hid[rows, :].astype(jnp.float32)
        r = lax.rsqrt(jnp.mean(h * h, axis=1, keepdims=True) + EPS)
        rinv[rows, :] = r
        toks[...] += jnp.sum(h, axis=0, keepdims=True)
        xbuf[me, rows, :] = (h * r * gain[...]).astype(jnp.bfloat16)
        return carry

    lax.fori_loop(0, tokens // 16, norm_rows, 0)
    pl.semaphore_wait(barrier, WAYS - 1 + planes - 1)

    pending = []

    def offset(h, du, dv):
        du, dv = du % 4, dv % 4
        return (du, dv) if h == 0 else (dv, du)

    def spot(h, du, dv):
        ox, oy = offset(h, du, dv)
        return oy * 4 + ox

    def rows_of(h, q):
        start = h * half
        if q is None:
            return pl.ds(start, half)
        return pl.ds(start + q * quarter, quarter)

    def send(h, du, dv, q, su, sv):
        block = at(*offset(h, du, dv))
        piece = xbuf.at[block, rows_of(h, q)]
        k = len([1 for kind, _ in pending if kind == 0])
        copy = pltpu.make_async_remote_copy(
            src_ref=piece,
            dst_ref=piece,
            send_sem=ag_s.at[k],
            recv_sem=ag_r.at[h, spot(h, du - su, dv - sv), q or 0],
            device_id={"exp": at(*offset(h, su, sv))},
            device_id_type=MESH,
        )
        copy.start()
        pending.append((0, copy))

    def share(h, du, dv):
        block = at(*offset(h, du, dv))
        piece = xbuf.at[block, rows_of(h, None)]
        k = spot(h, du, dv)
        copy = pltpu.make_async_remote_copy(
            src_ref=piece,
            dst_ref=piece,
            send_sem=pt_s.at[h, k],
            recv_sem=pt_r.at[h, k],
            device_id={"exp": at(0, 0, 1)},
            device_id_type=MESH,
        )
        copy.start()
        pending.append((1, copy))

    def arrive(h, du, dv, q):
        block = at(*offset(h, du, dv))
        piece = xbuf.at[block, rows_of(h, q)]
        pltpu.make_async_copy(piece, piece, ag_r.at[h, spot(h, du, dv), q or 0]).wait()

    for h in (0, 1):
        send(h, 0, 0, None, 1, 0)
        send(h, 0, 0, None, 3, 0)
    for h in (0, 1):
        send(h, 0, 0, None, 0, 1)
        send(h, 0, 0, None, 0, 3)
    for h in (0, 1):
        share(h, 0, 0)

    logits = dot(rout_t[...], xbuf[me], NT)
    experts = lax.broadcasted_iota(jnp.int32, (WAYS, tokens), 0)
    picked = ids_t[0:1, :] == experts
    for k in range(1, ids_t.shape[0]):
        picked = jnp.logical_or(picked, ids_t[k : k + 1, :] == experts)
    weights = jnp.where(picked, jnp.exp(logits), 0.0)
    gates = weights / jnp.sum(weights, axis=0, keepdims=True)
    gate_s[...] = gates
    gate_low = gates.astype(jnp.bfloat16).astype(jnp.float32)
    gsend[:, 0, :] = jnp.where(picked, gate_low, -1.0)
    before = (
        lax.broadcasted_iota(jnp.int32, (tokens, tokens), 0)
        < lax.broadcasted_iota(jnp.int32, (tokens, tokens), 1)
    ).astype(jnp.float32).astype(jnp.bfloat16)

    def rank_of(mask):
        place = dot(mask.astype(jnp.float32).astype(jnp.bfloat16), before, NN)
        return jnp.where(mask, place, -1.0)

    def to_all(source, target, which, put=None):
        def one(i, carry):
            e = lax.rem(me + i, WAYS)
            pltpu.make_async_remote_copy(
                src_ref=source(e),
                dst_ref=target.at[me] if put is None else target.at[put],
                send_sem=small_s.at[which],
                recv_sem=small_r.at[which],
                device_id={"exp": e},
                device_id_type=MESH,
            ).start()
            return carry

        lax.fori_loop(1, WAYS, one, 0)

    def from_all(target, which, count=WAYS - 1):
        block = target.at[pl.ds(0, count)]
        pltpu.make_async_copy(block, block, small_r.at[which]).wait()

    def sent_all(target, which, count=WAYS - 1):
        block = target.at[pl.ds(0, count)]
        pltpu.make_async_copy(block, block, small_s.at[which]).wait()

    def pair(e):
        return pl.ds(lax.div(e, 2) * 2, 2)

    to_all(lambda e: gsend.at[pair(e)], grecv, 0, pl.ds(me * 2, 2))
    grecv[pl.ds(me * 2, 2)] = gsend[pair(me)]

    for h in (0, 1):
        arrive(h, 3, 0, None)
        send(h, 3, 0, 0, 1, 0)
        send(h, 3, 0, None, 0, 1)
        send(h, 3, 0, None, 0, 3)
        arrive(h, 1, 0, None)
        send(h, 1, 0, 1, 3, 0)
        send(h, 1, 0, None, 0, 1)
        send(h, 1, 0, None, 0, 3)
    for h in (0, 1):
        arrive(h, 0, 3, None)
        send(h, 0, 3, 0, 0, 1)
        arrive(h, 0, 1, None)
        send(h, 0, 1, 1, 0, 3)
    for h in (0, 1):
        for du, dv in ((3, 0), (1, 0), (0, 3), (0, 1)):
            share(h, du, dv)

    from_all(grecv, 0, 2 * (WAYS - 1))
    everyone = grecv[:, 0, :]
    rk[:, 0, :] = rank_of(everyone >= 0.0)
    for load in loads[:2]:
        load.wait()
    slot = lax.broadcasted_iota(jnp.int32, (SLOTS, tokens), 0).astype(jnp.float32)

    def sources(group, sign=1):
        return [(at((sign * dx) % 4, (sign * dy) % 4, o), dx, dy, o) for dx, dy in group for o in (0, 1)]

    def forward(group):
        for dx, dy in group:
            for h in (0, 1):
                block = at(dx, dy, 1)
                piece = xbuf.at[block, rows_of(h, None)]
                pltpu.make_async_copy(piece, piece, pt_r.at[h, dy * 4 + dx]).wait()
        members = [s for s, _, _, _ in sources(group)]
        rows, gate_col = [], []
        for s in members:
            hit = slot == rk[s * 2 + core]
            one = jnp.where(hit, 1.0, 0.0)
            rows.append(dot(one.astype(jnp.bfloat16), xbuf[s], NN))
            gate_col.append(jnp.sum(jnp.where(hit, grecv[s * 2 + core], 0.0), axis=1, keepdims=True))
        xg[...] = jnp.concatenate(rows, axis=0).astype(jnp.bfloat16)
        weight = jnp.concatenate(gate_col, axis=0)
        step = min(256, units)

        def tile(n, carry):
            cols = pl.ds(pl.multiple_of(n * step, step), step)
            pre_gate = dot(xg[...], wg[:, cols], NN)
            pre_up = dot(xg[...], wu[:, cols], NN)
            sig = 1.0 / (1.0 + jnp.exp(-pre_gate))
            silu = pre_gate * sig
            slope = sig * (1.0 + pre_gate * (1.0 - sig))
            act = (silu * pre_up).astype(jnp.bfloat16).astype(jnp.float32)
            to_gate = weight * (pre_up * slope)
            to_up = weight * silu
            part = weight * act
            for i, s in enumerate(members):
                span = slice(i * SLOTS, (i + 1) * SLOTS)
                aref[s, :, cols] = to_gate[span]
                bref[s, :, cols] = to_up[span]
                actr[s, :, cols] = act[span]
                ppart[s, :, cols] = jnp.sum(part[span], axis=0, keepdims=True)
            return carry

        lax.fori_loop(0, units // step, tile, 0)

    forward(GROUPS[0])
    for h in (0, 1):
        for q in (0, 1):
            arrive(h, 2, 0, q)
            send(h, 2, 0, q, 0, 1)
            send(h, 2, 0, q, 0, 3)
        share(h, 2, 0)
    forward(GROUPS[1])
    for h in (0, 1):
        for du in (3, 1):
            arrive(h, du, 3, None)
            send(h, du, 3, 0, 0, 1)
            arrive(h, du, 1, None)
            send(h, du, 1, 1, 0, 3)
            share(h, du, 3)
            share(h, du, 1)
    forward(GROUPS[2])
    for h in (0, 1):
        arrive(h, 2, 3, 0)
        send(h, 2, 3, 0, 0, 1)
        arrive(h, 2, 1, 1)
        send(h, 2, 1, 1, 0, 3)
        arrive(h, 2, 3, 1)
        arrive(h, 2, 1, 0)
        share(h, 2, 3)
        share(h, 2, 1)
    forward(GROUPS[3])
    for h in (0, 1):
        arrive(h, 0, 2, 0)
        arrive(h, 0, 2, 1)
        share(h, 0, 2)
    forward(GROUPS[4])
    for h in (0, 1):
        for du in (3, 1):
            arrive(h, du, 2, 0)
            arrive(h, du, 2, 1)
            share(h, du, 2)
    forward(GROUPS[5])
    for h in (0, 1):
        arrive(h, 2, 2, 0)
        arrive(h, 2, 2, 1)
        share(h, 2, 2)
    forward(GROUPS[6])
    forward(GROUPS[7])

    loads[2].wait()
    xg[0 : 3 * WAYS, 0:units] = split3(ppart[:, 0, :])
    wide = min(256, width)

    def term_tile(n, carry):
        cols = pl.ds(pl.multiple_of(n * wide, wide), wide)
        t = dot(xg[0 : 3 * WAYS, 0:units], wd[:, cols], NN)
        tsend[:, 0, cols] = t[0:WAYS] + (t[WAYS : 2 * WAYS] + t[2 * WAYS : 3 * WAYS])
        return carry

    lax.fori_loop(0, width // wide, term_tile, 0)
    to_all(lambda e: tsend.at[e], trecv, 1)
    trecv[me] = tsend[me]
    from_all(trecv, 1)
    pooled = (toks[...] + jnp.sum(trecv[...], axis=0)) / tokens
    inv = lax.rsqrt(jnp.mean(pooled * pooled, axis=1, keepdims=True) + EPS)
    head_dir = fgain[...] * svec[...].astype(jnp.float32)
    score = jnp.sum(pooled * inv * head_dir, axis=1, keepdims=True)
    lean = jnp.mean(pooled * head_dir, axis=1, keepdims=True)
    head = inv * head_dir - pooled * (inv * inv * inv * lean)
    hbuf[me] = head
    zbuf[z] = jnp.broadcast_to(score, (1, zbuf.shape[2]))
    to_all(lambda e: hbuf.at[me], hbuf, 2)
    for i in range(1, planes):
        pltpu.make_async_remote_copy(
            src_ref=zbuf.at[z],
            dst_ref=zbuf.at[z],
            send_sem=small_s.at[3],
            recv_sem=small_r.at[3],
            device_id={"psg": lax.rem(z + i, planes)},
            device_id_type=MESH,
        ).start()
    from_all(hbuf, 2)
    h3[...] = split3(hbuf[:, 0, :])
    step = min(256, units)

    def near_tile(n, carry):
        cols = pl.ds(pl.multiple_of(n * step, step), step)
        t = dot(h3[...], wd[cols, :], NT)
        nref[:, 0, cols] = t[0:WAYS] + (t[WAYS : 2 * WAYS] + t[2 * WAYS : 3 * WAYS])
        return carry

    lax.fori_loop(0, units // step, near_tile, 0)

    for _, copy in pending:
        copy.wait_send()
    back = []

    def backward(group):
        members = sources(group)
        for i, (s, dx, dy, o) in enumerate(members):
            near = nref[s]
            gg = jnp.sum(actr[s] * near, axis=1, keepdims=True)
            ggsend[s] = jnp.sum(
                jnp.where(slot == rk[s * 2 + core], gg, 0.0), axis=0, keepdims=True
            )
        xg[:, 0:units] = jnp.concatenate(
            [aref[s] * nref[s] for s, _, _, _ in members], axis=0
        ).astype(jnp.bfloat16)
        xg[:, units : 2 * units] = jnp.concatenate(
            [bref[s] * nref[s] for s, _, _, _ in members], axis=0
        ).astype(jnp.bfloat16)

        def tile(n, carry):
            cols = pl.ds(pl.multiple_of(n * wide, wide), wide)
            g = dot(xg[:, 0:units], wg[cols, :], NT)
            g = g + dot(xg[:, units : 2 * units], wu[cols, :], NT)
            for i, (s, dx, dy, o) in enumerate(members):
                mine = g[i * SLOTS : (i + 1) * SLOTS].astype(jnp.bfloat16)
                if o:
                    psend[dy * 4 + dx, :, cols] = mine
                else:
                    xbuf[16 + dy * 4 + dx, 0:SLOTS, cols] = mine
            return carry

        lax.fori_loop(0, width // wide, tile, 0)
        for dx, dy in group:
            k = dy * 4 + dx
            copy = pltpu.make_async_remote_copy(
                src_ref=psend.at[k],
                dst_ref=precv.at[k],
                send_sem=pr_s.at[k],
                recv_sem=pr_r.at[k],
                device_id={"exp": at(0, 0, 1)},
                device_id_type=MESH,
            )
            copy.start()
            back.append(copy)

    def gather(group):
        hits = []
        for dx, dy in group:
            k = dy * 4 + dx
            pltpu.make_async_copy(precv.at[k], precv.at[k], pr_r.at[k]).wait()
            s = at(dx, dy)
            hits.append(
                jnp.concatenate(
                    [
                        jnp.where(slot == rk[s * 2 + core], 1.0, 0.0),
                        jnp.where(slot == rk[s * 2 + 1 - core], 1.0, 0.0),
                    ],
                    axis=0,
                ).astype(jnp.bfloat16)
            )

        def tile(n, carry):
            cols = pl.ds(pl.multiple_of(n * wide, wide), wide)
            for hit, (dx, dy) in zip(hits, group):
                k = dy * 4 + dx
                rows = jnp.concatenate(
                    [
                        xbuf[16 + k, 0:SLOTS, cols].astype(jnp.float32),
                        precv[k, :, cols].astype(jnp.float32),
                    ],
                    axis=0,
                ).astype(jnp.bfloat16)
                xbuf[k, :, cols] = dot(hit, rows, TN).astype(jnp.bfloat16)
            return carry

        lax.fori_loop(0, width // wide, tile, 0)

    def hand(h, k, q, to, landing, sem):
        copy = pltpu.make_async_remote_copy(
            src_ref=xbuf.at[k, rows_of(h, q)],
            dst_ref=landing,
            send_sem=tr_s.at[len(hops)],
            recv_sem=sem,
            device_id={"exp": to},
            device_id_type=MESH,
        )
        copy.start()
        hops.append(copy)

    hops = []

    def landed(ref, sem):
        pltpu.make_async_copy(ref, ref, sem).wait()

    def add(h, k, q, refs):
        start = h * half + (q or 0) * quarter
        count = half if q is None else quarter

        def rows16(i, carry):
            here = pl.ds(pl.multiple_of(start + i * 16, 16), 16)
            there = pl.ds(pl.multiple_of(i * 16, 16), 16)
            total = xbuf[k, here, :].astype(jnp.float32)
            for ref in refs:
                total = total + ref[there, :].astype(jnp.float32)
            xbuf[k, here, :] = total.astype(jnp.bfloat16)
            return carry

        lax.fori_loop(0, count // 16, rows16, 0)

    def relay(h, du, dv):
        k = spot(h, du, dv)
        if dv == 2:
            hand(h, k, 0, at(*offset(h, 0, 1)), vq.at[h, du, 0], vq_r.at[h, du, 0])
            hand(h, k, 1, at(*offset(h, 0, 3)), vq.at[h, du, 1], vq_r.at[h, du, 1])
            return
        if dv in (1, 3):
            side = 0 if dv == 1 else 1
            landed(vq.at[h, du, side], vq_r.at[h, du, side])
            add(h, k, side, [vq.at[h, du, side]])
            hand(h, k, None, at(*offset(h, 0, dv)), vf.at[h, du, side], vf_r.at[h, du, side])
            return
        for side in (0, 1):
            landed(vf.at[h, du, side], vf_r.at[h, du, side])
        if du == 0:
            for side in (0, 1):
                landed(uf.at[h, side], uf_r.at[h, side])

            def last(i, carry):
                here = pl.ds(pl.multiple_of(h * half + i * 16, 16), 16)
                there = pl.ds(pl.multiple_of(i * 16, 16), 16)
                total = xbuf[k, here, :].astype(jnp.float32)
                for side in (0, 1):
                    total = total + vf[h, du, side, there, :].astype(jnp.float32)
                    total = total + uf[h, side, there, :].astype(jnp.float32)
                acc[here, :] = total
                return carry

            lax.fori_loop(0, half // 16, last, 0)
            return
        add(h, k, None, [vf.at[h, du, 0], vf.at[h, du, 1]])
        if du == 2:
            hand(h, k, 0, at(*offset(h, 1, 0)), uq.at[h, 0], uq_r.at[h, 0])
            hand(h, k, 1, at(*offset(h, 3, 0)), uq.at[h, 1], uq_r.at[h, 1])
            return
        side = 0 if du == 1 else 1
        landed(uq.at[h, side], uq_r.at[h, side])
        add(h, k, side, [uq.at[h, side]])
        hand(h, k, None, at(*offset(h, du, 0)), uf.at[h, side], uf_r.at[h, side])

    for j, group in enumerate(BACK_GROUPS):
        backward(group)
        if j:
            gather(BACK_GROUPS[j - 1])
            for step_of in RELAYS[j - 1]:
                relay(*step_of)
    to_all(lambda e: ggsend.at[e], gown, 4)
    gown[me] = ggsend[me]
    gather(BACK_GROUPS[-1])
    for step_of in RELAYS[-1][:2]:
        relay(*step_of)

    from_all(zbuf, 3, planes - 1)
    eye_r = lax.broadcasted_iota(jnp.int32, (planes, planes), 0)
    eye_c = lax.broadcasted_iota(jnp.int32, (planes, planes), 1)
    eye = eye_r == eye_c

    def column(row):
        return jnp.sum(jnp.where(eye, row, 0.0), axis=1, keepdims=True)

    g_row = grades[...].astype(jnp.float32)
    g_col = column(g_row)
    s_col = zbuf[:, 0, 0:1]
    s_row = jnp.sum(jnp.where(eye, s_col, 0.0), axis=0, keepdims=True)
    ln2 = 0.6931471805599453
    d_row = ln2 / jnp.log(2.0 + ranks[...].astype(jnp.float32))
    d_col = column(d_row)
    worth_row = jnp.exp2(g_row)
    worth_col = column(worth_row)
    ahead = jnp.logical_or(g_row > g_col, jnp.logical_and(g_row == g_col, eye_c < eye_r))
    ideal = jnp.sum(jnp.where(ahead, 1.0, 0.0), axis=1, keepdims=True)
    ideal_gain = jnp.sum((worth_col - 1.0) * ln2 / jnp.log(2.0 + ideal), axis=0, keepdims=True)
    swap = jnp.abs((worth_col - worth_row) * (d_col - d_row)) / ideal_gain
    swap = jnp.where(g_col > g_row, swap, 0.0)
    margin = s_col - s_row
    soft = jnp.maximum(-margin, 0.0) + jnp.log(1.0 + jnp.exp(-jnp.abs(margin)))
    loss_o[0] = jnp.sum(swap * soft)
    pull = swap / (1.0 + jnp.exp(margin))
    d_own = jnp.sum(jnp.where(eye_c == z, pull, 0.0) - jnp.where(eye_r == z, pull, 0.0))
    score_o[0, 0] = jnp.sum(score)
    scale = d_own * (LOSS_SCALE / tokens)

    from_all(gown, 4)
    gate_grad = gown[:, 0, :]
    gates = gate_s[...]
    d_logit = gates * (gate_grad - jnp.sum(gates * gate_grad, axis=0, keepdims=True))
    d_logit = split3(d_logit)
    rout3 = jnp.concatenate([rout_t[...]] * 3, axis=0)
    for step_of in RELAYS[-1][2:]:
        relay(*step_of)
    acc[...] += dot(d_logit, rout3, TN)
    head = hbuf[me]

    def finish(i, carry):
        rows = pl.ds(pl.multiple_of(i * 16, 16), 16)
        h = hid[rows, :].astype(jnp.float32)
        r = rinv[rows, :]
        scaled = acc[rows, :] * gain[...]
        lean = jnp.mean(h * scaled, axis=1, keepdims=True)
        full = r * scaled - h * (r * r * r * lean) + head
        out_o[rows, :] = (full * scale).astype(jnp.bfloat16)
        return carry

    lax.fori_loop(0, tokens // 16, finish, 0)
    for copy in back + hops:
        copy.wait_send()
    sent_all(grecv, 0, 2 * (WAYS - 1))
    sent_all(tsend, 1)
    sent_all(hbuf, 2)
    sent_all(zbuf, 3, planes - 1)
    sent_all(gown, 4)


def local(
    hidden,
    norm_gain,
    router,
    gate_proj,
    up_proj,
    down_proj,
    final_gain,
    score_vector,
    expert_ids,
    grades,
    passage_ranks,
):
    tokens, width = hidden.shape[2:]
    units = gate_proj.shape[2]
    planes = lax.axis_size("psg")
    f32, bf16 = jnp.float32, jnp.bfloat16
    vmem = pl.BlockSpec(memory_space=pltpu.VMEM)
    any_space = pl.BlockSpec(memory_space=pl.ANY)
    smem = pl.BlockSpec(memory_space=pltpu.SMEM)
    scratch = [
        pltpu.VMEM((WAYS, tokens, width), bf16),
        pltpu.VMEM((width, units), bf16),
        pltpu.VMEM((width, units), bf16),
        pltpu.VMEM((units, width), bf16),
        pltpu.VMEM((WAYS, tokens), f32),
        pltpu.VMEM((tokens, 1), f32),
        pltpu.VMEM((1, width), f32),
        pltpu.VMEM((WAYS, 1, tokens), f32),
        pltpu.VMEM((2 * WAYS, 1, tokens), f32),
        pltpu.VMEM((2 * WAYS, 1, tokens), f32),
        pltpu.VMEM((4 * SLOTS, max(width, 2 * units)), bf16),
        pltpu.VMEM((WAYS, SLOTS, units), f32),
        pltpu.VMEM((WAYS, SLOTS, units), f32),
        pltpu.VMEM((WAYS, SLOTS, units), f32),
        pltpu.VMEM((WAYS, 1, units), f32),
        pltpu.VMEM((WAYS, 1, width), f32),
        pltpu.VMEM((WAYS, 1, width), f32),
        pltpu.VMEM((WAYS, 1, width), f32),
        pltpu.VMEM((3 * WAYS, width), bf16),
        pltpu.VMEM((WAYS, 1, units), f32),
        pltpu.VMEM((planes, 1, tokens), f32),
        pltpu.VMEM((16, SLOTS, width), bf16),
        pltpu.VMEM((16, SLOTS, width), bf16),
        pltpu.VMEM((2, 4, 2, tokens // 4, width), bf16),
        pltpu.VMEM((2, 4, 2, tokens // 2, width), bf16),
        pltpu.VMEM((2, 2, tokens // 4, width), bf16),
        pltpu.VMEM((2, 2, tokens // 2, width), bf16),
        pltpu.VMEM((WAYS, 1, tokens), f32),
        pltpu.VMEM((WAYS, 1, tokens), f32),
        pltpu.VMEM((tokens, width), f32),
        pltpu.SemaphoreType.DMA((3,)),
        pltpu.SemaphoreType.DMA((44,)),
        pltpu.SemaphoreType.DMA((2, 16, 2)),
        pltpu.SemaphoreType.DMA((2, 16)),
        pltpu.SemaphoreType.DMA((2, 16)),
        pltpu.SemaphoreType.DMA((5,)),
        pltpu.SemaphoreType.DMA((5,)),
        pltpu.SemaphoreType.DMA((16,)),
        pltpu.SemaphoreType.DMA((16,)),
        pltpu.SemaphoreType.DMA((40,)),
        pltpu.SemaphoreType.DMA((2, 4, 2)),
        pltpu.SemaphoreType.DMA((2, 4, 2)),
        pltpu.SemaphoreType.DMA((2, 2)),
        pltpu.SemaphoreType.DMA((2, 2)),
    ]
    loss, score, grad = pl.pallas_call(
        kernel,
        out_shape=(
            jax.ShapeDtypeStruct((1,), f32),
            jax.ShapeDtypeStruct((1, 1), f32),
            jax.ShapeDtypeStruct((tokens, width), bf16),
        ),
        in_specs=[vmem] * 8 + [any_space] * 3,
        out_specs=(smem, smem, vmem),
        scratch_shapes=scratch,
        compiler_params=pltpu.CompilerParams(
            collective_id=0, has_side_effects=True, vmem_limit_bytes=62 * 1024 * 1024
        ),
        name="expert_block",
    )(
        hidden.reshape(tokens, width),
        expert_ids.reshape(tokens, -1).T,
        norm_gain.reshape(1, width),
        router.T,
        final_gain.reshape(1, width),
        score_vector.reshape(1, width),
        grades,
        passage_ranks,
        gate_proj[0],
        up_proj[0],
        down_proj[0],
    )
    return loss, score, grad.reshape(1, 1, tokens, width)


def solution(mesh):
    placed = (
        P("exp", "psg", None, None),
        P(),
        P(),
        P("exp", None, None),
        P("exp", None, None),
        P("exp", None, None),
        P(),
        P(),
        P("exp", "psg", None, None),
        P("exp", None),
        P("exp", None),
    )
    return jax.shard_map(
        local,
        mesh=mesh,
        in_specs=placed,
        out_specs=(P("exp"), P("exp", "psg"), P("exp", "psg", None, None)),
        check_vma=False,
    )
```

```python
import jax
import jax.numpy as jnp
from jax import lax
from jax.experimental import pallas as pl
from jax.experimental.pallas import tpu as pltpu
from jax.sharding import PartitionSpec as P

MESH = pl.DeviceIdType.MESH
EPS = 1e-06
LOSS_SCALE = 256.0
SLOTS = 40
WAYS = 32
NN = (((1,), (0,)), ((), ()))
NT = (((1,), (1,)), ((), ()))
TN = (((0,), (0,)), ((), ()))

GROUPS = (
    ((0, 0), (1, 0), (3, 0), (0, 1)),
    ((0, 3), (1, 1), (1, 3), (3, 1)),
    ((3, 3), (2, 0), (0, 2)),
    ((2, 1), (2, 3), (1, 2), (3, 2)),
    ((2, 2),),
)
BACK = (
    (((2, 2), (1, 2)), (), ((0, 2, 2), (1, 2, 2), (0, 1, 2))),
    (((2, 1), (3, 2)), ((1, 2, 1),), ((1, 1, 2), (0, 3, 2), (0, 2, 1), (1, 2, 3))),
    (
        ((2, 3), (2, 0), (0, 2), (1, 1)),
        (),
        ((1, 3, 2), (1, 0, 2), (0, 0, 2), (0, 2, 3), (0, 1, 1), (1, 1, 1), (1, 2, 0)),
    ),
    (
        ((1, 3), (3, 1), (3, 3), (0, 0)),
        ((0, 2, 0),),
        ((0, 1, 3), (1, 3, 1), (0, 3, 1), (1, 1, 3), (0, 3, 3), (1, 3, 3)),
    ),
    (
        ((1, 0), (0, 1), (3, 0), (0, 3)),
        (),
        (
            (1, 0, 1), (1, 0, 3), (0, 0, 1), (0, 0, 3),
            (0, 1, 0), (1, 1, 0), (0, 3, 0), (1, 3, 0),
        ),
    ),
)


def dot(a, b, dims):
    return lax.dot_general(a, b, dims, preferred_element_type=jnp.float32)


def split3(v):
    hi = v.astype(jnp.bfloat16).astype(jnp.float32)
    rest = v - hi
    mid = rest.astype(jnp.bfloat16).astype(jnp.float32)
    low = rest - mid
    return jnp.concatenate([hi, mid, low], axis=0).astype(jnp.bfloat16)


def kernel(
    hid, ids_t, gain, rout_t, fgain, svec, grades, ranks, wg_hbm, wu_hbm, wd_hbm,
    stat_o, out_o,
    xbuf, wg, wu, wd, gate_s, rinv, toks, gsend, grecv, rk,
    xg, aref, bref, actr, ppart, stage, tsend, trecv, hbuf, headrow, h3, nref, zbuf,
    psend, precv, vq, vf, uq, uf, ggsend, gown, acc,
    wsem, ag_s, ag_r, pt_s, pt_r, small_s, small_r, pr_s, pr_r, tr_s, vq_r, vf_r, uq_r, uf_r,
):
    tokens, width = hid.shape
    units = wg.shape[1]
    half, quarter = tokens // 2, tokens // 4
    planes = zbuf.shape[0]
    me = lax.axis_index("exp")
    z = lax.axis_index("psg")
    core = lax.rem(me, 2)
    cx = lax.rem(lax.div(me, 2), 4)
    cy = lax.div(me, 8)

    def at(dx, dy, other=0):
        side = (1 - core) if other else core
        return (lax.rem(cy + dy, 4) * 4 + lax.rem(cx + dx, 4)) * 2 + side

    barrier = pltpu.get_barrier_semaphore()

    def greet(i, carry):
        pl.semaphore_signal(
            barrier, inc=1, device_id={"exp": lax.rem(me + i, WAYS)}, device_id_type=MESH
        )
        return carry

    lax.fori_loop(1, WAYS, greet, 0)
    for i in range(1, planes):
        pl.semaphore_signal(
            barrier, inc=1, device_id={"psg": lax.rem(z + i, planes)}, device_id_type=MESH
        )
    loads = [
        pltpu.make_async_copy(wg_hbm, wg, wsem.at[0]),
        pltpu.make_async_copy(wu_hbm, wu, wsem.at[1]),
        pltpu.make_async_copy(wd_hbm, wd, wsem.at[2]),
    ]
    for load in loads:
        load.start()

    toks[...] = jnp.zeros_like(toks)

    def norm_rows(i, carry):
        rows = pl.ds(pl.multiple_of(i * 16, 16), 16)
        h = hid[rows, :].astype(jnp.float32)
        r = lax.rsqrt(jnp.mean(h * h, axis=1, keepdims=True) + EPS)
        rinv[rows, :] = r
        toks[...] += jnp.sum(h, axis=0, keepdims=True)
        xbuf[me, rows, :] = (h * r * gain[...]).astype(jnp.bfloat16)
        return carry

    lax.fori_loop(0, tokens // 16, norm_rows, 0)
    pl.semaphore_wait(barrier, WAYS - 1 + planes - 1)

    pending = []

    def offset(h, du, dv):
        du, dv = du % 4, dv % 4
        return (du, dv) if h == 0 else (dv, du)

    def spot(h, du, dv):
        ox, oy = offset(h, du, dv)
        return oy * 4 + ox

    def rows_of(h, q):
        start = h * half
        if q is None:
            return pl.ds(start, half)
        return pl.ds(start + q * quarter, quarter)

    def send(h, du, dv, q, su, sv):
        block = at(*offset(h, du, dv))
        piece = xbuf.at[block, rows_of(h, q)]
        k = len([1 for kind, _ in pending if kind == 0])
        copy = pltpu.make_async_remote_copy(
            src_ref=piece,
            dst_ref=piece,
            send_sem=ag_s.at[k],
            recv_sem=ag_r.at[h, spot(h, du - su, dv - sv), q or 0],
            device_id={"exp": at(*offset(h, su, sv))},
            device_id_type=MESH,
        )
        copy.start()
        pending.append((0, copy))

    def share(h, du, dv):
        block = at(*offset(h, du, dv))
        piece = xbuf.at[block, rows_of(h, None)]
        k = spot(h, du, dv)
        copy = pltpu.make_async_remote_copy(
            src_ref=piece,
            dst_ref=piece,
            send_sem=pt_s.at[h, k],
            recv_sem=pt_r.at[h, k],
            device_id={"exp": at(0, 0, 1)},
            device_id_type=MESH,
        )
        copy.start()
        pending.append((1, copy))

    def arrive(h, du, dv, q):
        block = at(*offset(h, du, dv))
        piece = xbuf.at[block, rows_of(h, q)]
        pltpu.make_async_copy(piece, piece, ag_r.at[h, spot(h, du, dv), q or 0]).wait()

    for h in (0, 1):
        send(h, 0, 0, None, 1, 0)
        send(h, 0, 0, None, 3, 0)
    for h in (0, 1):
        send(h, 0, 0, None, 0, 1)
        send(h, 0, 0, None, 0, 3)
    for h in (0, 1):
        share(h, 0, 0)

    logits = dot(rout_t[...], xbuf[me], NT)
    experts = lax.broadcasted_iota(jnp.int32, (WAYS, tokens), 0)
    picked = ids_t[0:1, :] == experts
    for k in range(1, ids_t.shape[0]):
        picked = jnp.logical_or(picked, ids_t[k : k + 1, :] == experts)
    weights = jnp.where(picked, jnp.exp(logits), 0.0)
    gates = weights / jnp.sum(weights, axis=0, keepdims=True)
    gate_s[...] = gates
    gate_low = gates.astype(jnp.bfloat16).astype(jnp.float32)
    gsend[:, 0, :] = jnp.where(picked, gate_low, -1.0)
    before = (
        lax.broadcasted_iota(jnp.int32, (tokens, tokens), 0)
        < lax.broadcasted_iota(jnp.int32, (tokens, tokens), 1)
    ).astype(jnp.float32).astype(jnp.bfloat16)

    def rank_of(mask):
        place = dot(mask.astype(jnp.float32).astype(jnp.bfloat16), before, NN)
        return jnp.where(mask, place, -1.0)

    def to_all(source, target, which, put=None):
        def one(i, carry):
            e = lax.rem(me + i, WAYS)
            pltpu.make_async_remote_copy(
                src_ref=source(e),
                dst_ref=target.at[me] if put is None else target.at[put],
                send_sem=small_s.at[which],
                recv_sem=small_r.at[which],
                device_id={"exp": e},
                device_id_type=MESH,
            ).start()
            return carry

        lax.fori_loop(1, WAYS, one, 0)

    def from_all(target, which, count=WAYS - 1):
        block = target.at[pl.ds(0, count)]
        pltpu.make_async_copy(block, block, small_r.at[which]).wait()

    def sent_all(target, which, count=WAYS - 1):
        block = target.at[pl.ds(0, count)]
        pltpu.make_async_copy(block, block, small_s.at[which]).wait()

    def pair(e):
        return pl.ds(lax.div(e, 2) * 2, 2)

    to_all(lambda e: gsend.at[pair(e)], grecv, 0, pl.ds(me * 2, 2))
    grecv[pl.ds(me * 2, 2)] = gsend[pair(me)]

    for h in (0, 1):
        arrive(h, 3, 0, None)
        send(h, 3, 0, 0, 1, 0)
        send(h, 3, 0, None, 0, 1)
        send(h, 3, 0, None, 0, 3)
        arrive(h, 1, 0, None)
        send(h, 1, 0, 1, 3, 0)
        send(h, 1, 0, None, 0, 1)
        send(h, 1, 0, None, 0, 3)
    for h in (0, 1):
        arrive(h, 0, 3, None)
        send(h, 0, 3, 0, 0, 1)
        arrive(h, 0, 1, None)
        send(h, 0, 1, 1, 0, 3)
    for h in (0, 1):
        for du, dv in ((3, 0), (1, 0), (0, 3), (0, 1)):
            share(h, du, dv)

    from_all(grecv, 0, 2 * (WAYS - 1))
    everyone = grecv[:, 0, :]
    rk[:, 0, :] = rank_of(everyone >= 0.0)
    for load in loads[:2]:
        load.wait()
    slot = lax.broadcasted_iota(jnp.int32, (SLOTS, tokens), 0).astype(jnp.float32)

    def sources(group, sign=1):
        return [(at((sign * dx) % 4, (sign * dy) % 4, o), dx, dy, o) for dx, dy in group for o in (0, 1)]

    def forward(group):
        for dx, dy in group:
            for h in (0, 1):
                block = at(dx, dy, 1)
                piece = xbuf.at[block, rows_of(h, None)]
                pltpu.make_async_copy(piece, piece, pt_r.at[h, dy * 4 + dx]).wait()
        members = [s for s, _, _, _ in sources(group)]
        rows, gate_col = [], []
        for s in members:
            hit = slot == rk[s * 2 + core]
            one = jnp.where(hit, 1.0, 0.0)
            rows.append(dot(one.astype(jnp.bfloat16), xbuf[s], NN))
            gate_col.append(jnp.sum(jnp.where(hit, grecv[s * 2 + core], 0.0), axis=1, keepdims=True))
        count = len(members) * SLOTS
        xg[0:count, 0:width] = jnp.concatenate(rows, axis=0).astype(jnp.bfloat16)
        weight = jnp.concatenate(gate_col, axis=0)
        step = min(256, units)

        def tile(n, carry):
            cols = pl.ds(pl.multiple_of(n * step, step), step)
            pre_gate = dot(xg[0:count, 0:width], wg[:, cols], NN)
            pre_up = dot(xg[0:count, 0:width], wu[:, cols], NN)
            sig = 1.0 / (1.0 + jnp.exp(-pre_gate))
            silu = pre_gate * sig
            slope = sig * (1.0 + pre_gate * (1.0 - sig))
            act = (silu * pre_up).astype(jnp.bfloat16).astype(jnp.float32)
            to_gate = weight * (pre_up * slope)
            to_up = weight * silu
            part = weight * act
            for i, s in enumerate(members):
                span = slice(i * SLOTS, (i + 1) * SLOTS)
                aref[s, :, cols] = to_gate[span]
                bref[s, :, cols] = to_up[span]
                actr[s, :, cols] = act[span]
                ppart[s, :, cols] = jnp.sum(part[span], axis=0, keepdims=True)
            return carry

        lax.fori_loop(0, units // step, tile, 0)

    forward(GROUPS[0])
    for h in (0, 1):
        for q in (0, 1):
            arrive(h, 2, 0, q)
            send(h, 2, 0, q, 0, 1)
            send(h, 2, 0, q, 0, 3)
        share(h, 2, 0)
    for h in (0, 1):
        for du in (3, 1):
            arrive(h, du, 3, None)
            send(h, du, 3, 0, 0, 1)
            arrive(h, du, 1, None)
            send(h, du, 1, 1, 0, 3)
            share(h, du, 3)
            share(h, du, 1)
    forward(GROUPS[1])
    for h in (0, 1):
        arrive(h, 2, 3, 0)
        send(h, 2, 3, 0, 0, 1)
        arrive(h, 2, 1, 1)
        send(h, 2, 1, 1, 0, 3)
        arrive(h, 2, 3, 1)
        arrive(h, 2, 1, 0)
        share(h, 2, 3)
        share(h, 2, 1)
    for h in (0, 1):
        arrive(h, 0, 2, 0)
        arrive(h, 0, 2, 1)
        share(h, 0, 2)
    forward(GROUPS[2])
    for h in (0, 1):
        for du in (3, 1):
            arrive(h, du, 2, 0)
            arrive(h, du, 2, 1)
            share(h, du, 2)
    forward(GROUPS[3])
    for h in (0, 1):
        arrive(h, 2, 2, 0)
        arrive(h, 2, 2, 1)
        share(h, 2, 2)
    forward(GROUPS[4])

    loads[2].wait()
    xg[0 : 3 * WAYS, 0:units] = split3(ppart[:, 0, :])
    wide = min(256, width)
    lanes = stage.shape[2]
    blocks = width // lanes
    for n in range(width // wide):
        cols = slice(n * wide, (n + 1) * wide)
        t = dot(xg[0 : 3 * WAYS, 0:units], wd[:, cols], NN)
        t = t[0:WAYS] + (t[WAYS : 2 * WAYS] + t[2 * WAYS : 3 * WAYS])
        for j in range(wide // lanes):
            stage[:, n * (wide // lanes) + j, :] = t[:, j * lanes : (j + 1) * lanes]
    tsend[...] = stage[...].astype(jnp.bfloat16)
    to_all(lambda e: tsend.at[e], trecv, 1)
    trecv[me] = tsend[me]
    own = jnp.concatenate(
        [toks[:, j * lanes : (j + 1) * lanes] for j in range(blocks)], axis=0
    )
    head_dir = fgain[...] * svec[...].astype(jnp.float32)
    from_all(trecv, 1)
    pooled = (own + jnp.sum(trecv[...].astype(jnp.float32), axis=0)) / tokens

    def total(v):
        return jnp.sum(jnp.sum(v, axis=1, keepdims=True), axis=0, keepdims=True)

    inv = lax.rsqrt(total(pooled * pooled) / width + EPS)
    score = total(pooled * inv * head_dir)
    lean = total(pooled * head_dir) / width
    head = inv * head_dir - pooled * (inv * inv * inv * lean)
    hbuf[me] = head.astype(jnp.bfloat16)
    zbuf[z] = jnp.broadcast_to(score, (1, zbuf.shape[2]))
    to_all(lambda e: hbuf.at[me], hbuf, 2)
    for i in range(1, planes):
        pltpu.make_async_remote_copy(
            src_ref=zbuf.at[z],
            dst_ref=zbuf.at[z],
            send_sem=small_s.at[3],
            recv_sem=small_r.at[3],
            device_id={"psg": lax.rem(z + i, planes)},
            device_id_type=MESH,
        ).start()
    for j in range(blocks):
        headrow[:, j * lanes : (j + 1) * lanes] = head[j : j + 1]
    from_all(hbuf, 2)
    stage[...] = hbuf[...].astype(jnp.float32)
    for j in range(blocks):
        h3[:, j * lanes : (j + 1) * lanes] = stage[:, j, :].astype(jnp.bfloat16)
    step = min(256, units)

    def near_tile(n, carry):
        cols = pl.ds(pl.multiple_of(n * step, step), step)
        nref[:, 0, cols] = dot(h3[...], wd[cols, :], NT)
        return carry

    lax.fori_loop(0, units // step, near_tile, 0)

    for _, copy in pending:
        copy.wait_send()
    back = []

    def backward(group):
        members = sources(group)
        for i, (s, dx, dy, o) in enumerate(members):
            near = nref[s]
            gg = jnp.sum(actr[s] * near, axis=1, keepdims=True)
            ggsend[s] = jnp.sum(
                jnp.where(slot == rk[s * 2 + core], gg, 0.0), axis=0, keepdims=True
            )
        count = len(members) * SLOTS
        xg[0:count, 0:units] = jnp.concatenate(
            [aref[s] * nref[s] for s, _, _, _ in members], axis=0
        ).astype(jnp.bfloat16)
        xg[0:count, units : 2 * units] = jnp.concatenate(
            [bref[s] * nref[s] for s, _, _, _ in members], axis=0
        ).astype(jnp.bfloat16)

        def tile(n, carry):
            cols = pl.ds(pl.multiple_of(n * wide, wide), wide)
            g = dot(xg[0:count, 0:units], wg[cols, :], NT)
            g = g + dot(xg[0:count, units : 2 * units], wu[cols, :], NT)
            for i, (s, dx, dy, o) in enumerate(members):
                mine = g[i * SLOTS : (i + 1) * SLOTS].astype(jnp.bfloat16)
                if o:
                    psend[dy * 4 + dx, :, cols] = mine
                else:
                    xbuf[16 + dy * 4 + dx, 0:SLOTS, cols] = mine
            return carry

        lax.fori_loop(0, width // wide, tile, 0)
        for dx, dy in group:
            k = dy * 4 + dx
            copy = pltpu.make_async_remote_copy(
                src_ref=psend.at[k],
                dst_ref=precv.at[k],
                send_sem=pr_s.at[k],
                recv_sem=pr_r.at[k],
                device_id={"exp": at(0, 0, 1)},
                device_id_type=MESH,
            )
            copy.start()
            back.append(copy)

    def gather(group):
        hits = []
        for dx, dy in group:
            s = at(dx, dy)
            for r in (s * 2 + core, s * 2 + 1 - core):
                hits.append(jnp.where(slot == rk[r], 1.0, 0.0).T.astype(jnp.bfloat16))
        for dx, dy in group:
            k = dy * 4 + dx
            pltpu.make_async_copy(precv.at[k], precv.at[k], pr_r.at[k]).wait()

        def tile(n, carry):
            cols = pl.ds(pl.multiple_of(n * wide, wide), wide)
            for i, (dx, dy) in enumerate(group):
                k = dy * 4 + dx
                rows = dot(hits[2 * i], xbuf[16 + k, 0:SLOTS, cols], NN)
                rows = rows + dot(hits[2 * i + 1], precv[k, :, cols], NN)
                xbuf[k, :, cols] = rows.astype(jnp.bfloat16)
            return carry

        lax.fori_loop(0, width // wide, tile, 0)

    def hand(h, k, q, to, landing, sem):
        copy = pltpu.make_async_remote_copy(
            src_ref=xbuf.at[k, rows_of(h, q)],
            dst_ref=landing,
            send_sem=tr_s.at[len(hops)],
            recv_sem=sem,
            device_id={"exp": to},
            device_id_type=MESH,
        )
        copy.start()
        hops.append(copy)

    hops = []

    def landed(ref, sem):
        pltpu.make_async_copy(ref, ref, sem).wait()

    def add(h, k, q, refs):
        start = h * half + (q or 0) * quarter
        count = half if q is None else quarter

        def rows16(i, carry):
            here = pl.ds(pl.multiple_of(start + i * 16, 16), 16)
            there = pl.ds(pl.multiple_of(i * 16, 16), 16)
            total = xbuf[k, here, :].astype(jnp.float32)
            for ref in refs:
                total = total + ref[there, :].astype(jnp.float32)
            xbuf[k, here, :] = total.astype(jnp.bfloat16)
            return carry

        lax.fori_loop(0, count // 16, rows16, 0)

    def relay(h, du, dv):
        k = spot(h, du, dv)
        if dv == 2:
            hand(h, k, 0, at(*offset(h, 0, 1)), vq.at[h, du, 0], vq_r.at[h, du, 0])
            hand(h, k, 1, at(*offset(h, 0, 3)), vq.at[h, du, 1], vq_r.at[h, du, 1])
            return
        if dv in (1, 3):
            side = 0 if dv == 1 else 1
            landed(vq.at[h, du, side], vq_r.at[h, du, side])
            add(h, k, side, [vq.at[h, du, side]])
            hand(h, k, None, at(*offset(h, 0, dv)), vf.at[h, du, side], vf_r.at[h, du, side])
            return
        for side in (0, 1):
            landed(vf.at[h, du, side], vf_r.at[h, du, side])
        if du == 0:
            for side in (0, 1):
                landed(uf.at[h, side], uf_r.at[h, side])

            def last(i, carry):
                here = pl.ds(pl.multiple_of(h * half + i * 16, 16), 16)
                there = pl.ds(pl.multiple_of(i * 16, 16), 16)
                total = xbuf[k, here, :].astype(jnp.float32)
                for side in (0, 1):
                    total = total + vf[h, du, side, there, :].astype(jnp.float32)
                    total = total + uf[h, side, there, :].astype(jnp.float32)
                acc[here, :] = total
                return carry

            lax.fori_loop(0, half // 16, last, 0)
            return
        add(h, k, None, [vf.at[h, du, 0], vf.at[h, du, 1]])
        if du == 2:
            hand(h, k, 0, at(*offset(h, 1, 0)), uq.at[h, 0], uq_r.at[h, 0])
            hand(h, k, 1, at(*offset(h, 3, 0)), uq.at[h, 1], uq_r.at[h, 1])
            return
        side = 0 if du == 1 else 1
        landed(uq.at[h, side], uq_r.at[h, side])
        add(h, k, side, [uq.at[h, side]])
        hand(h, k, None, at(*offset(h, du, 0)), uf.at[h, side], uf_r.at[h, side])

    for group, early, late in BACK:
        backward(group)
        for step_of in early:
            relay(*step_of)
        gather(group)
        for step_of in late:
            relay(*step_of)
    to_all(lambda e: ggsend.at[e], gown, 4)
    gown[me] = ggsend[me]

    from_all(zbuf, 3, planes - 1)
    eye_r = lax.broadcasted_iota(jnp.int32, (planes, planes), 0)
    eye_c = lax.broadcasted_iota(jnp.int32, (planes, planes), 1)
    eye = eye_r == eye_c

    def column(row):
        return jnp.sum(jnp.where(eye, row, 0.0), axis=1, keepdims=True)

    g_row = grades[...].astype(jnp.float32)
    g_col = column(g_row)
    s_col = zbuf[:, 0, 0:1]
    s_row = jnp.sum(jnp.where(eye, s_col, 0.0), axis=0, keepdims=True)
    ln2 = 0.6931471805599453
    d_row = ln2 / jnp.log(2.0 + ranks[...].astype(jnp.float32))
    d_col = column(d_row)
    worth_row = jnp.exp2(g_row)
    worth_col = column(worth_row)
    ahead = jnp.logical_or(g_row > g_col, jnp.logical_and(g_row == g_col, eye_c < eye_r))
    ideal = jnp.sum(jnp.where(ahead, 1.0, 0.0), axis=1, keepdims=True)
    ideal_gain = jnp.sum((worth_col - 1.0) * ln2 / jnp.log(2.0 + ideal), axis=0, keepdims=True)
    swap = jnp.abs((worth_col - worth_row) * (d_col - d_row)) / ideal_gain
    swap = jnp.where(g_col > g_row, swap, 0.0)
    margin = s_col - s_row
    soft = jnp.maximum(-margin, 0.0) + jnp.log(1.0 + jnp.exp(-jnp.abs(margin)))
    loss = total(swap * soft)
    pull = swap / (1.0 + jnp.exp(margin))
    d_own = jnp.sum(jnp.where(eye_c == z, pull, 0.0) - jnp.where(eye_r == z, pull, 0.0))
    spot_of = lax.broadcasted_iota(jnp.int32, stat_o.shape, 1)
    stat_o[...] = jnp.where(spot_of == 0, loss, score)
    scale = d_own * (LOSS_SCALE / tokens)

    from_all(gown, 4)
    gate_grad = gown[:, 0, :]
    gates = gate_s[...]
    d_logit = gates * (gate_grad - jnp.sum(gates * gate_grad, axis=0, keepdims=True))
    d_logit = split3(d_logit)
    rout3 = jnp.concatenate([rout_t[...]] * 3, axis=0)
    relay(0, 0, 0)
    relay(1, 0, 0)
    acc[...] += dot(d_logit, rout3, TN)
    head = headrow[...]

    def finish(i, carry):
        rows = pl.ds(pl.multiple_of(i * 16, 16), 16)
        h = hid[rows, :].astype(jnp.float32)
        r = rinv[rows, :]
        scaled = acc[rows, :] * gain[...]
        lean = jnp.mean(h * scaled, axis=1, keepdims=True)
        full = r * scaled - h * (r * r * r * lean) + head
        out_o[rows, :] = (full * scale).astype(jnp.bfloat16)
        return carry

    lax.fori_loop(0, tokens // 16, finish, 0)
    for copy in back + hops:
        copy.wait_send()
    sent_all(grecv, 0, 2 * (WAYS - 1))
    sent_all(tsend, 1)
    sent_all(hbuf, 2)
    sent_all(zbuf, 3, planes - 1)
    sent_all(gown, 4)


def local(
    hidden,
    norm_gain,
    router,
    gate_proj,
    up_proj,
    down_proj,
    final_gain,
    score_vector,
    expert_ids,
    grades,
    passage_ranks,
):
    tokens, width = hidden.shape[2:]
    units = gate_proj.shape[2]
    planes = lax.axis_size("psg")
    f32, bf16 = jnp.float32, jnp.bfloat16
    vmem = pl.BlockSpec(memory_space=pltpu.VMEM)
    any_space = pl.BlockSpec(memory_space=pl.ANY)
    scratch = [
        pltpu.VMEM((WAYS, tokens, width), bf16),
        pltpu.VMEM((width, units), bf16),
        pltpu.VMEM((width, units), bf16),
        pltpu.VMEM((units, width), bf16),
        pltpu.VMEM((WAYS, tokens), f32),
        pltpu.VMEM((tokens, 1), f32),
        pltpu.VMEM((1, width), f32),
        pltpu.VMEM((WAYS, 1, tokens), f32),
        pltpu.VMEM((2 * WAYS, 1, tokens), f32),
        pltpu.VMEM((2 * WAYS, 1, tokens), f32),
        pltpu.VMEM((8 * SLOTS, max(width, 2 * units)), bf16),
        pltpu.VMEM((WAYS, SLOTS, units), f32),
        pltpu.VMEM((WAYS, SLOTS, units), f32),
        pltpu.VMEM((WAYS, SLOTS, units), f32),
        pltpu.VMEM((WAYS, 1, units), f32),
        pltpu.VMEM((WAYS, width // 128, 128), f32),
        pltpu.VMEM((WAYS, width // 128, 128), bf16),
        pltpu.VMEM((WAYS, width // 128, 128), bf16),
        pltpu.VMEM((WAYS, width // 128, 128), bf16),
        pltpu.VMEM((1, width), f32),
        pltpu.VMEM((WAYS, width), bf16),
        pltpu.VMEM((WAYS, 1, units), f32),
        pltpu.VMEM((planes, 1, tokens), f32),
        pltpu.VMEM((16, SLOTS, width), bf16),
        pltpu.VMEM((16, SLOTS, width), bf16),
        pltpu.VMEM((2, 4, 2, tokens // 4, width), bf16),
        pltpu.VMEM((2, 4, 2, tokens // 2, width), bf16),
        pltpu.VMEM((2, 2, tokens // 4, width), bf16),
        pltpu.VMEM((2, 2, tokens // 2, width), bf16),
        pltpu.VMEM((WAYS, 1, tokens), f32),
        pltpu.VMEM((WAYS, 1, tokens), f32),
        pltpu.VMEM((tokens, width), f32),
        pltpu.SemaphoreType.DMA((3,)),
        pltpu.SemaphoreType.DMA((44,)),
        pltpu.SemaphoreType.DMA((2, 16, 2)),
        pltpu.SemaphoreType.DMA((2, 16)),
        pltpu.SemaphoreType.DMA((2, 16)),
        pltpu.SemaphoreType.DMA((5,)),
        pltpu.SemaphoreType.DMA((5,)),
        pltpu.SemaphoreType.DMA((16,)),
        pltpu.SemaphoreType.DMA((16,)),
        pltpu.SemaphoreType.DMA((40,)),
        pltpu.SemaphoreType.DMA((2, 4, 2)),
        pltpu.SemaphoreType.DMA((2, 4, 2)),
        pltpu.SemaphoreType.DMA((2, 2)),
        pltpu.SemaphoreType.DMA((2, 2)),
    ]
    stat, grad = pl.pallas_call(
        kernel,
        out_shape=(
            jax.ShapeDtypeStruct((1, 128), f32),
            jax.ShapeDtypeStruct((tokens, width), bf16),
        ),
        in_specs=[vmem] * 8 + [any_space] * 3,
        out_specs=(vmem, vmem),
        scratch_shapes=scratch,
        compiler_params=pltpu.CompilerParams(
            collective_id=0, has_side_effects=True, vmem_limit_bytes=62 * 1024 * 1024
        ),
        name="expert_block",
    )(
        hidden.reshape(tokens, width),
        expert_ids.reshape(tokens, -1).T,
        norm_gain.reshape(1, width),
        router.T,
        final_gain.reshape(width // 128, 128),
        score_vector.reshape(width // 128, 128),
        grades,
        passage_ranks,
        gate_proj[0],
        up_proj[0],
        down_proj[0],
    )
    return stat[0, 0:1], stat[0:1, 1:2], grad.reshape(1, 1, tokens, width)


def solution(mesh):
    placed = (
        P("exp", "psg", None, None),
        P(),
        P(),
        P("exp", None, None),
        P("exp", None, None),
        P("exp", None, None),
        P(),
        P(),
        P("exp", "psg", None, None),
        P("exp", None),
        P("exp", None),
    )
    return jax.shard_map(
        local,
        mesh=mesh,
        in_specs=placed,
        out_specs=(P("exp"), P("exp", "psg"), P("exp", "psg", None, None)),
        check_vma=False,
    )
```

```python
import jax
import jax.numpy as jnp
from jax import lax
from jax.experimental import pallas as pl
from jax.experimental.pallas import tpu as pltpu
from jax.sharding import PartitionSpec as P

MESH = pl.DeviceIdType.MESH
EPS = 1e-06
LOSS_SCALE = 256.0
SLOTS = 40
WAYS = 32
NN = (((1,), (0,)), ((), ()))
NT = (((1,), (1,)), ((), ()))
TN = (((0,), (0,)), ((), ()))

GROUPS = (
    ((0, 0), (1, 0), (3, 0), (0, 1)),
    ((0, 3), (1, 1), (1, 3), (3, 1)),
    ((3, 3), (2, 0), (0, 2)),
    ((3, 2), (2, 3)),
    ((1, 2), (2, 1)),
    ((2, 2),),
)
BACK = (
    (((2, 2), (1, 2)), (), ((0, 2, 2), (1, 2, 2), (0, 1, 2))),
    (((2, 1), (3, 2)), ((1, 2, 1),), ((1, 1, 2), (0, 3, 2), (0, 2, 1), (1, 2, 3))),
    (
        ((2, 3), (2, 0), (0, 2), (1, 1)),
        (),
        ((1, 3, 2), (1, 0, 2), (0, 0, 2), (0, 2, 3), (0, 1, 1), (1, 1, 1), (1, 2, 0)),
    ),
    (
        ((1, 3), (3, 1), (3, 3)),
        ((0, 2, 0),),
        ((0, 1, 3), (1, 3, 1), (0, 3, 1), (1, 1, 3), (0, 3, 3), (1, 3, 3)),
    ),
    (
        ((1, 0), (0, 1), (3, 0), (0, 3)),
        (),
        (
            (1, 0, 1), (1, 0, 3), (0, 0, 1), (0, 0, 3),
            (0, 1, 0), (1, 1, 0), (0, 3, 0), (1, 3, 0),
        ),
    ),
)


def dot(a, b, dims):
    return lax.dot_general(a, b, dims, preferred_element_type=jnp.float32)


def split3(v):
    hi = v.astype(jnp.bfloat16).astype(jnp.float32)
    rest = v - hi
    mid = rest.astype(jnp.bfloat16).astype(jnp.float32)
    low = rest - mid
    return jnp.concatenate([hi, mid, low], axis=0).astype(jnp.bfloat16)


def kernel(
    hid, ids_t, gain, rout_t, fgain, svec, grades, ranks, wg_hbm, wu_hbm, wd_hbm,
    stat_o, out_o,
    xbuf, wg, wu, wd, gate_s, rinv, toks, gsend, grecv, rk,
    xg, aref, bref, actr, ppart, stage, tsend, trecv, hbuf, headrow, h3, nref, zbuf,
    psend, precv, vq, vf, uq, uf, ggsend, gown, acc,
    wsem, ag_s, ag_r, pt_s, pt_r, small_s, small_r, pr_s, pr_r, tr_s, vq_r, vf_r, uq_r, uf_r,
):
    tokens, width = hid.shape
    units = wg.shape[1]
    half, quarter = tokens // 2, tokens // 4
    planes = zbuf.shape[0]
    me = lax.axis_index("exp")
    z = lax.axis_index("psg")
    core = lax.rem(me, 2)
    cx = lax.rem(lax.div(me, 2), 4)
    cy = lax.div(me, 8)

    def at(dx, dy, other=0):
        side = (1 - core) if other else core
        return (lax.rem(cy + dy, 4) * 4 + lax.rem(cx + dx, 4)) * 2 + side

    barrier = pltpu.get_barrier_semaphore()

    def greet(i, carry):
        pl.semaphore_signal(
            barrier, inc=1, device_id={"exp": lax.rem(me + i, WAYS)}, device_id_type=MESH
        )
        return carry

    lax.fori_loop(1, WAYS, greet, 0)
    for i in range(1, planes):
        pl.semaphore_signal(
            barrier, inc=1, device_id={"psg": lax.rem(z + i, planes)}, device_id_type=MESH
        )
    loads = [
        pltpu.make_async_copy(wg_hbm, wg, wsem.at[0]),
        pltpu.make_async_copy(wu_hbm, wu, wsem.at[1]),
        pltpu.make_async_copy(wd_hbm, wd, wsem.at[2]),
    ]
    for load in loads:
        load.start()

    toks[...] = jnp.zeros_like(toks)

    def norm_rows(i, carry):
        rows = pl.ds(pl.multiple_of(i * 16, 16), 16)
        h = hid[rows, :].astype(jnp.float32)
        r = lax.rsqrt(jnp.mean(h * h, axis=1, keepdims=True) + EPS)
        rinv[rows, :] = r
        toks[...] += jnp.sum(h, axis=0, keepdims=True)
        xbuf[me, rows, :] = (h * r * gain[...]).astype(jnp.bfloat16)
        return carry

    lax.fori_loop(0, tokens // 16, norm_rows, 0)
    pl.semaphore_wait(barrier, WAYS - 1 + planes - 1)

    pending = []

    def offset(h, du, dv):
        du, dv = du % 4, dv % 4
        return (du, dv) if h == 0 else (dv, du)

    def spot(h, du, dv):
        ox, oy = offset(h, du, dv)
        return oy * 4 + ox

    def rows_of(h, q):
        start = h * half
        if q is None:
            return pl.ds(start, half)
        return pl.ds(start + q * quarter, quarter)

    def send(h, du, dv, q, su, sv):
        block = at(*offset(h, du, dv))
        piece = xbuf.at[block, rows_of(h, q)]
        k = len([1 for kind, _ in pending if kind == 0])
        copy = pltpu.make_async_remote_copy(
            src_ref=piece,
            dst_ref=piece,
            send_sem=ag_s.at[k],
            recv_sem=ag_r.at[h, spot(h, du - su, dv - sv), q or 0],
            device_id={"exp": at(*offset(h, su, sv))},
            device_id_type=MESH,
        )
        copy.start()
        pending.append((0, copy))

    def share(h, du, dv):
        block = at(*offset(h, du, dv))
        piece = xbuf.at[block, rows_of(h, None)]
        k = spot(h, du, dv)
        copy = pltpu.make_async_remote_copy(
            src_ref=piece,
            dst_ref=piece,
            send_sem=pt_s.at[h, k],
            recv_sem=pt_r.at[h, k],
            device_id={"exp": at(0, 0, 1)},
            device_id_type=MESH,
        )
        copy.start()
        pending.append((1, copy))

    def arrive(h, du, dv, q):
        block = at(*offset(h, du, dv))
        piece = xbuf.at[block, rows_of(h, q)]
        pltpu.make_async_copy(piece, piece, ag_r.at[h, spot(h, du, dv), q or 0]).wait()

    for h in (0, 1):
        send(h, 0, 0, None, 1, 0)
        send(h, 0, 0, None, 3, 0)
    for h in (0, 1):
        send(h, 0, 0, None, 0, 1)
        send(h, 0, 0, None, 0, 3)
    for h in (0, 1):
        share(h, 0, 0)

    logits = dot(rout_t[...], xbuf[me], NT)
    experts = lax.broadcasted_iota(jnp.int32, (WAYS, tokens), 0)
    picked = ids_t[0:1, :] == experts
    for k in range(1, ids_t.shape[0]):
        picked = jnp.logical_or(picked, ids_t[k : k + 1, :] == experts)
    weights = jnp.where(picked, jnp.exp(logits), 0.0)
    gates = weights / jnp.sum(weights, axis=0, keepdims=True)
    gate_s[...] = gates
    gate_low = gates.astype(jnp.bfloat16).astype(jnp.float32)
    gsend[:, 0, :] = jnp.where(picked, gate_low, -1.0)
    before = (
        lax.broadcasted_iota(jnp.int32, (tokens, tokens), 0)
        < lax.broadcasted_iota(jnp.int32, (tokens, tokens), 1)
    ).astype(jnp.float32).astype(jnp.bfloat16)

    def rank_of(mask):
        place = dot(mask.astype(jnp.float32).astype(jnp.bfloat16), before, NN)
        return jnp.where(mask, place, -1.0)

    def to_all(source, target, which, put=None):
        def one(i, carry):
            e = lax.rem(me + i, WAYS)
            pltpu.make_async_remote_copy(
                src_ref=source(e),
                dst_ref=target.at[me] if put is None else target.at[put],
                send_sem=small_s.at[which],
                recv_sem=small_r.at[which],
                device_id={"exp": e},
                device_id_type=MESH,
            ).start()
            return carry

        lax.fori_loop(1, WAYS, one, 0)

    def from_all(target, which, count=WAYS - 1):
        block = target.at[pl.ds(0, count)]
        pltpu.make_async_copy(block, block, small_r.at[which]).wait()

    def sent_all(target, which, count=WAYS - 1):
        block = target.at[pl.ds(0, count)]
        pltpu.make_async_copy(block, block, small_s.at[which]).wait()

    def pair(e):
        return pl.ds(lax.div(e, 2) * 2, 2)

    to_all(lambda e: gsend.at[pair(e)], grecv, 0, pl.ds(me * 2, 2))
    grecv[pl.ds(me * 2, 2)] = gsend[pair(me)]

    for h in (0, 1):
        arrive(h, 3, 0, None)
        send(h, 3, 0, 0, 1, 0)
        send(h, 3, 0, None, 0, 1)
        send(h, 3, 0, None, 0, 3)
        arrive(h, 1, 0, None)
        send(h, 1, 0, 1, 3, 0)
        send(h, 1, 0, None, 0, 1)
        send(h, 1, 0, None, 0, 3)
    for h in (0, 1):
        arrive(h, 0, 3, None)
        send(h, 0, 3, 0, 0, 1)
        arrive(h, 0, 1, None)
        send(h, 0, 1, 1, 0, 3)
    for h in (0, 1):
        for du, dv in ((3, 0), (1, 0), (0, 3), (0, 1)):
            share(h, du, dv)

    from_all(grecv, 0, 2 * (WAYS - 1))
    everyone = grecv[:, 0, :]
    rk[:, 0, :] = rank_of(everyone >= 0.0)
    for load in loads[:2]:
        load.wait()
    slot = lax.broadcasted_iota(jnp.int32, (SLOTS, tokens), 0).astype(jnp.float32)

    def sources(group, sign=1):
        return [(at((sign * dx) % 4, (sign * dy) % 4, o), dx, dy, o) for dx, dy in group for o in (0, 1)]

    def forward(group):
        for dx, dy in group:
            for h in (0, 1):
                block = at(dx, dy, 1)
                piece = xbuf.at[block, rows_of(h, None)]
                pltpu.make_async_copy(piece, piece, pt_r.at[h, dy * 4 + dx]).wait()
        members = [s for s, _, _, _ in sources(group)]
        rows, gate_col = [], []
        for s in members:
            hit = slot == rk[s * 2 + core]
            one = jnp.where(hit, 1.0, 0.0)
            rows.append(dot(one.astype(jnp.bfloat16), xbuf[s], NN))
            gate_col.append(jnp.sum(jnp.where(hit, grecv[s * 2 + core], 0.0), axis=1, keepdims=True))
        count = len(members) * SLOTS
        xg[0:count, 0:width] = jnp.concatenate(rows, axis=0).astype(jnp.bfloat16)
        weight = jnp.concatenate(gate_col, axis=0)
        step = min(256, units)

        def tile(n, carry):
            cols = pl.ds(pl.multiple_of(n * step, step), step)
            pre_gate = dot(xg[0:count, 0:width], wg[:, cols], NN)
            pre_up = dot(xg[0:count, 0:width], wu[:, cols], NN)
            sig = 1.0 / (1.0 + jnp.exp(-pre_gate))
            silu = pre_gate * sig
            slope = sig * (1.0 + pre_gate * (1.0 - sig))
            act = (silu * pre_up).astype(jnp.bfloat16).astype(jnp.float32)
            to_gate = weight * (pre_up * slope)
            to_up = weight * silu
            part = weight * act
            for i, s in enumerate(members):
                span = slice(i * SLOTS, (i + 1) * SLOTS)
                aref[s, :, cols] = to_gate[span]
                bref[s, :, cols] = to_up[span]
                actr[s, :, cols] = act[span]
                ppart[s, :, cols] = jnp.sum(part[span], axis=0, keepdims=True)
            return carry

        lax.fori_loop(0, units // step, tile, 0)

    forward(GROUPS[0])
    for h in (0, 1):
        for q in (0, 1):
            arrive(h, 2, 0, q)
            send(h, 2, 0, q, 0, 1)
            send(h, 2, 0, q, 0, 3)
        share(h, 2, 0)
    for h in (0, 1):
        for du in (3, 1):
            arrive(h, du, 3, None)
            send(h, du, 3, 0, 0, 1)
            arrive(h, du, 1, None)
            send(h, du, 1, 1, 0, 3)
            share(h, du, 3)
            share(h, du, 1)
    forward(GROUPS[1])
    for h in (0, 1):
        arrive(h, 2, 3, 0)
        send(h, 2, 3, 0, 0, 1)
        arrive(h, 2, 1, 1)
        send(h, 2, 1, 1, 0, 3)
        arrive(h, 2, 3, 1)
        arrive(h, 2, 1, 0)
        share(h, 2, 3)
        share(h, 2, 1)
    for h in (0, 1):
        arrive(h, 0, 2, 0)
        arrive(h, 0, 2, 1)
        share(h, 0, 2)
    forward(GROUPS[2])
    for du, group in ((3, GROUPS[3]), (1, GROUPS[4])):
        for h in (0, 1):
            arrive(h, du, 2, 0)
            arrive(h, du, 2, 1)
            share(h, du, 2)
        forward(group)
    for h in (0, 1):
        arrive(h, 2, 2, 0)
        arrive(h, 2, 2, 1)
        share(h, 2, 2)
    forward(GROUPS[5])

    loads[2].wait()
    xg[0 : 3 * WAYS, 0:units] = split3(ppart[:, 0, :])
    wide = min(256, width)
    lanes = stage.shape[2]
    blocks = width // lanes
    for n in range(width // wide):
        cols = slice(n * wide, (n + 1) * wide)
        t = dot(xg[0 : 3 * WAYS, 0:units], wd[:, cols], NN)
        t = t[0:WAYS] + (t[WAYS : 2 * WAYS] + t[2 * WAYS : 3 * WAYS])
        for j in range(wide // lanes):
            stage[:, n * (wide // lanes) + j, :] = t[:, j * lanes : (j + 1) * lanes]
    tsend[...] = stage[...].astype(jnp.bfloat16)
    to_all(lambda e: tsend.at[e], trecv, 1)
    trecv[me] = tsend[me]
    own = jnp.concatenate(
        [toks[:, j * lanes : (j + 1) * lanes] for j in range(blocks)], axis=0
    )
    head_dir = fgain[...] * svec[...].astype(jnp.float32)
    from_all(trecv, 1)
    pooled = (own + jnp.sum(trecv[...].astype(jnp.float32), axis=0)) / tokens

    def total(v):
        return jnp.sum(jnp.sum(v, axis=1, keepdims=True), axis=0, keepdims=True)

    inv = lax.rsqrt(total(pooled * pooled) / width + EPS)
    score = total(pooled * inv * head_dir)
    lean = total(pooled * head_dir) / width
    head = inv * head_dir - pooled * (inv * inv * inv * lean)
    hbuf[me] = head.astype(jnp.bfloat16)
    zbuf[z] = jnp.broadcast_to(score, (1, zbuf.shape[2]))
    to_all(lambda e: hbuf.at[me], hbuf, 2)
    for i in range(1, planes):
        pltpu.make_async_remote_copy(
            src_ref=zbuf.at[z],
            dst_ref=zbuf.at[z],
            send_sem=small_s.at[3],
            recv_sem=small_r.at[3],
            device_id={"psg": lax.rem(z + i, planes)},
            device_id_type=MESH,
        ).start()
    for j in range(blocks):
        headrow[:, j * lanes : (j + 1) * lanes] = head[j : j + 1]
    from_all(hbuf, 2)
    stage[...] = hbuf[...].astype(jnp.float32)
    for j in range(blocks):
        h3[:, j * lanes : (j + 1) * lanes] = stage[:, j, :].astype(jnp.bfloat16)
    step = min(256, units)

    def near_tile(n, carry):
        cols = pl.ds(pl.multiple_of(n * step, step), step)
        nref[:, 0, cols] = dot(h3[...], wd[cols, :], NT)
        return carry

    lax.fori_loop(0, units // step, near_tile, 0)

    for _, copy in pending:
        copy.wait_send()
    back = []
    turns = width // wide // 2

    def backward(group):
        members = sources(group)
        count = len(members) * SLOTS
        xg[0:count, 0:units] = jnp.concatenate(
            [aref[s] * nref[s] for s, _, _, _ in members], axis=0
        ).astype(jnp.bfloat16)
        xg[0:count, units : 2 * units] = jnp.concatenate(
            [bref[s] * nref[s] for s, _, _, _ in members], axis=0
        ).astype(jnp.bfloat16)

        def tile(n, carry):
            cols = pl.ds(pl.multiple_of(n * wide, wide), wide)
            g = dot(xg[0:count, 0:units], wg[cols, :], NT)
            g = g + dot(xg[0:count, units : 2 * units], wu[cols, :], NT)
            for i, (s, dx, dy, o) in enumerate(members):
                mine = g[i * SLOTS : (i + 1) * SLOTS].astype(jnp.bfloat16)
                if o:
                    psend[dy * 4 + dx, :, cols] = mine
                else:
                    xbuf[16 + dy * 4 + dx, 0:SLOTS, cols] = mine
            return carry

        for c in (0, 1):
            lax.fori_loop(c * turns, (c + 1) * turns, tile, 0)
            for dx, dy in group:
                k = dy * 4 + dx
                cols = pl.ds(c * (width // 2), width // 2)
                copy = pltpu.make_async_remote_copy(
                    src_ref=psend.at[k, :, cols],
                    dst_ref=precv.at[k, :, cols],
                    send_sem=pr_s.at[c, k],
                    recv_sem=pr_r.at[c, k],
                    device_id={"exp": at(0, 0, 1)},
                    device_id_type=MESH,
                )
                copy.start()
                back.append(copy)

    def gather(group):
        hits = []
        for dx, dy in group:
            s = at(dx, dy)
            for r in (s * 2 + core, s * 2 + 1 - core):
                hits.append(jnp.where(slot == rk[r], 1.0, 0.0).T.astype(jnp.bfloat16))
        def tile(n, carry):
            cols = pl.ds(pl.multiple_of(n * wide, wide), wide)
            for i, (dx, dy) in enumerate(group):
                k = dy * 4 + dx
                rows = dot(hits[2 * i], xbuf[16 + k, 0:SLOTS, cols], NN)
                rows = rows + dot(hits[2 * i + 1], precv[k, :, cols], NN)
                xbuf[k, :, cols] = rows.astype(jnp.bfloat16)
            return carry

        for c in (0, 1):
            for dx, dy in group:
                k = dy * 4 + dx
                piece = precv.at[k, :, pl.ds(c * (width // 2), width // 2)]
                pltpu.make_async_copy(piece, piece, pr_r.at[c, k]).wait()
            lax.fori_loop(c * turns, (c + 1) * turns, tile, 0)

    def hand(h, k, q, to, landing, sem):
        copy = pltpu.make_async_remote_copy(
            src_ref=xbuf.at[k, rows_of(h, q)],
            dst_ref=landing,
            send_sem=tr_s.at[len(hops)],
            recv_sem=sem,
            device_id={"exp": to},
            device_id_type=MESH,
        )
        copy.start()
        hops.append(copy)

    hops = []

    def landed(ref, sem):
        pltpu.make_async_copy(ref, ref, sem).wait()

    def add(h, k, q, refs):
        start = h * half + (q or 0) * quarter
        count = half if q is None else quarter

        def rows16(i, carry):
            here = pl.ds(pl.multiple_of(start + i * 16, 16), 16)
            there = pl.ds(pl.multiple_of(i * 16, 16), 16)
            total = xbuf[k, here, :].astype(jnp.float32)
            for ref in refs:
                total = total + ref[there, :].astype(jnp.float32)
            xbuf[k, here, :] = total.astype(jnp.bfloat16)
            return carry

        lax.fori_loop(0, count // 16, rows16, 0)

    def relay(h, du, dv):
        k = spot(h, du, dv)
        if dv == 2:
            hand(h, k, 0, at(*offset(h, 0, 1)), vq.at[h, du, 0], vq_r.at[h, du, 0])
            hand(h, k, 1, at(*offset(h, 0, 3)), vq.at[h, du, 1], vq_r.at[h, du, 1])
            return
        if dv in (1, 3):
            side = 0 if dv == 1 else 1
            landed(vq.at[h, du, side], vq_r.at[h, du, side])
            add(h, k, side, [vq.at[h, du, side]])
            hand(h, k, None, at(*offset(h, 0, dv)), vf.at[h, du, side], vf_r.at[h, du, side])
            return
        for side in (0, 1):
            landed(vf.at[h, du, side], vf_r.at[h, du, side])
        if du == 0:
            for side in (0, 1):
                landed(uf.at[h, side], uf_r.at[h, side])

            def last(i, carry):
                here = pl.ds(pl.multiple_of(h * half + i * 16, 16), 16)
                there = pl.ds(pl.multiple_of(i * 16, 16), 16)
                total = acc[here, :] + xbuf[k, here, :].astype(jnp.float32)
                for side in (0, 1):
                    total = total + vf[h, du, side, there, :].astype(jnp.float32)
                    total = total + uf[h, side, there, :].astype(jnp.float32)
                acc[here, :] = total
                return carry

            lax.fori_loop(0, half // 16, last, 0)
            return
        add(h, k, None, [vf.at[h, du, 0], vf.at[h, du, 1]])
        if du == 2:
            hand(h, k, 0, at(*offset(h, 1, 0)), uq.at[h, 0], uq_r.at[h, 0])
            hand(h, k, 1, at(*offset(h, 3, 0)), uq.at[h, 1], uq_r.at[h, 1])
            return
        side = 0 if du == 1 else 1
        landed(uq.at[h, side], uq_r.at[h, side])
        add(h, k, side, [uq.at[h, side]])
        hand(h, k, None, at(*offset(h, du, 0)), uf.at[h, side], uf_r.at[h, side])

    for group, early, late in BACK:
        backward(group)
        for step_of in early:
            relay(*step_of)
        gather(group)
        for step_of in late:
            relay(*step_of)

    def gate_gradient(s, carry):
        gg = jnp.sum(actr[s] * nref[s], axis=1, keepdims=True)
        ggsend[s] = jnp.sum(
            jnp.where(slot == rk[s * 2 + core], gg, 0.0), axis=0, keepdims=True
        )
        return carry

    lax.fori_loop(0, WAYS, gate_gradient, 0)
    to_all(lambda e: ggsend.at[e], gown, 4)
    gown[me] = ggsend[me]
    backward(((0, 0),))
    gather(((0, 0),))

    from_all(zbuf, 3, planes - 1)
    eye_r = lax.broadcasted_iota(jnp.int32, (planes, planes), 0)
    eye_c = lax.broadcasted_iota(jnp.int32, (planes, planes), 1)
    eye = eye_r == eye_c

    def column(row):
        return jnp.sum(jnp.where(eye, row, 0.0), axis=1, keepdims=True)

    g_row = grades[...].astype(jnp.float32)
    g_col = column(g_row)
    s_col = zbuf[:, 0, 0:1]
    s_row = jnp.sum(jnp.where(eye, s_col, 0.0), axis=0, keepdims=True)
    ln2 = 0.6931471805599453
    d_row = ln2 / jnp.log(2.0 + ranks[...].astype(jnp.float32))
    d_col = column(d_row)
    worth_row = jnp.exp2(g_row)
    worth_col = column(worth_row)
    ahead = jnp.logical_or(g_row > g_col, jnp.logical_and(g_row == g_col, eye_c < eye_r))
    ideal = jnp.sum(jnp.where(ahead, 1.0, 0.0), axis=1, keepdims=True)
    ideal_gain = jnp.sum((worth_col - 1.0) * ln2 / jnp.log(2.0 + ideal), axis=0, keepdims=True)
    swap = jnp.abs((worth_col - worth_row) * (d_col - d_row)) / ideal_gain
    swap = jnp.where(g_col > g_row, swap, 0.0)
    margin = s_col - s_row
    soft = jnp.maximum(-margin, 0.0) + jnp.log(1.0 + jnp.exp(-jnp.abs(margin)))
    loss = total(swap * soft)
    pull = swap / (1.0 + jnp.exp(margin))
    d_own = jnp.sum(jnp.where(eye_c == z, pull, 0.0) - jnp.where(eye_r == z, pull, 0.0))
    spot_of = lax.broadcasted_iota(jnp.int32, stat_o.shape, 1)
    stat_o[...] = jnp.where(spot_of == 0, loss, score)
    scale = d_own * (LOSS_SCALE / tokens)

    from_all(gown, 4)
    gate_grad = gown[:, 0, :]
    gates = gate_s[...]
    d_logit = gates * (gate_grad - jnp.sum(gates * gate_grad, axis=0, keepdims=True))
    d_logit = split3(d_logit)
    rout3 = jnp.concatenate([rout_t[...]] * 3, axis=0)
    acc[...] = dot(d_logit, rout3, TN)
    head = headrow[...]

    def finish(i, carry):
        rows = pl.ds(pl.multiple_of(i * 16, 16), 16)
        h = hid[rows, :].astype(jnp.float32)
        r = rinv[rows, :]
        scaled = acc[rows, :] * gain[...]
        lean = jnp.mean(h * scaled, axis=1, keepdims=True)
        full = r * scaled - h * (r * r * r * lean) + head
        out_o[rows, :] = (full * scale).astype(jnp.bfloat16)
        return carry

    for h in (0, 1):
        relay(h, 0, 0)
        lax.fori_loop(h * half // 16, (h + 1) * half // 16, finish, 0)
    for copy in back + hops:
        copy.wait_send()
    sent_all(grecv, 0, 2 * (WAYS - 1))
    sent_all(tsend, 1)
    sent_all(hbuf, 2)
    sent_all(zbuf, 3, planes - 1)
    sent_all(gown, 4)


def local(
    hidden,
    norm_gain,
    router,
    gate_proj,
    up_proj,
    down_proj,
    final_gain,
    score_vector,
    expert_ids,
    grades,
    passage_ranks,
):
    tokens, width = hidden.shape[2:]
    units = gate_proj.shape[2]
    planes = lax.axis_size("psg")
    f32, bf16 = jnp.float32, jnp.bfloat16
    vmem = pl.BlockSpec(memory_space=pltpu.VMEM)
    any_space = pl.BlockSpec(memory_space=pl.ANY)
    scratch = [
        pltpu.VMEM((WAYS, tokens, width), bf16),
        pltpu.VMEM((width, units), bf16),
        pltpu.VMEM((width, units), bf16),
        pltpu.VMEM((units, width), bf16),
        pltpu.VMEM((WAYS, tokens), f32),
        pltpu.VMEM((tokens, 1), f32),
        pltpu.VMEM((1, width), f32),
        pltpu.VMEM((WAYS, 1, tokens), f32),
        pltpu.VMEM((2 * WAYS, 1, tokens), f32),
        pltpu.VMEM((2 * WAYS, 1, tokens), f32),
        pltpu.VMEM((8 * SLOTS, max(width, 2 * units)), bf16),
        pltpu.VMEM((WAYS, SLOTS, units), f32),
        pltpu.VMEM((WAYS, SLOTS, units), f32),
        pltpu.VMEM((WAYS, SLOTS, units), f32),
        pltpu.VMEM((WAYS, 1, units), f32),
        pltpu.VMEM((WAYS, width // 128, 128), f32),
        pltpu.VMEM((WAYS, width // 128, 128), bf16),
        pltpu.VMEM((WAYS, width // 128, 128), bf16),
        pltpu.VMEM((WAYS, width // 128, 128), bf16),
        pltpu.VMEM((1, width), f32),
        pltpu.VMEM((WAYS, width), bf16),
        pltpu.VMEM((WAYS, 1, units), f32),
        pltpu.VMEM((planes, 1, tokens), f32),
        pltpu.VMEM((16, SLOTS, width), bf16),
        pltpu.VMEM((16, SLOTS, width), bf16),
        pltpu.VMEM((2, 4, 2, tokens // 4, width), bf16),
        pltpu.VMEM((2, 4, 2, tokens // 2, width), bf16),
        pltpu.VMEM((2, 2, tokens // 4, width), bf16),
        pltpu.VMEM((2, 2, tokens // 2, width), bf16),
        pltpu.VMEM((WAYS, 1, tokens), f32),
        pltpu.VMEM((WAYS, 1, tokens), f32),
        pltpu.VMEM((tokens, width), f32),
        pltpu.SemaphoreType.DMA((3,)),
        pltpu.SemaphoreType.DMA((44,)),
        pltpu.SemaphoreType.DMA((2, 16, 2)),
        pltpu.SemaphoreType.DMA((2, 16)),
        pltpu.SemaphoreType.DMA((2, 16)),
        pltpu.SemaphoreType.DMA((5,)),
        pltpu.SemaphoreType.DMA((5,)),
        pltpu.SemaphoreType.DMA((2, 16)),
        pltpu.SemaphoreType.DMA((2, 16)),
        pltpu.SemaphoreType.DMA((40,)),
        pltpu.SemaphoreType.DMA((2, 4, 2)),
        pltpu.SemaphoreType.DMA((2, 4, 2)),
        pltpu.SemaphoreType.DMA((2, 2)),
        pltpu.SemaphoreType.DMA((2, 2)),
    ]
    stat, grad = pl.pallas_call(
        kernel,
        out_shape=(
            jax.ShapeDtypeStruct((1, 128), f32),
            jax.ShapeDtypeStruct((tokens, width), bf16),
        ),
        in_specs=[vmem] * 8 + [any_space] * 3,
        out_specs=(vmem, vmem),
        scratch_shapes=scratch,
        compiler_params=pltpu.CompilerParams(
            collective_id=0, has_side_effects=True, vmem_limit_bytes=62 * 1024 * 1024
        ),
        name="expert_block",
    )(
        hidden.reshape(tokens, width),
        expert_ids.reshape(tokens, -1).T,
        norm_gain.reshape(1, width),
        router.T,
        final_gain.reshape(width // 128, 128),
        score_vector.reshape(width // 128, 128),
        grades,
        passage_ranks,
        gate_proj[0],
        up_proj[0],
        down_proj[0],
    )
    return stat[0, 0:1], stat[0:1, 1:2], grad.reshape(1, 1, tokens, width)


def solution(mesh):
    placed = (
        P("exp", "psg", None, None),
        P(),
        P(),
        P("exp", None, None),
        P("exp", None, None),
        P("exp", None, None),
        P(),
        P(),
        P("exp", "psg", None, None),
        P("exp", None),
        P("exp", None),
    )
    return jax.shard_map(
        local,
        mesh=mesh,
        in_specs=placed,
        out_specs=(P("exp"), P("exp", "psg"), P("exp", "psg", None, None)),
        check_vma=False,
    )
```

```python
import jax
import jax.numpy as jnp
from jax import lax
from jax.experimental import pallas as pl
from jax.experimental.pallas import tpu as pltpu
from jax.sharding import PartitionSpec as P

MESH = pl.DeviceIdType.MESH
EPS = 1e-06
LOSS_SCALE = 256.0
SLOTS = 40
WAYS = 32
NN = (((1,), (0,)), ((), ()))
NT = (((1,), (1,)), ((), ()))
TN = (((0,), (0,)), ((), ()))

GROUPS = (
    ((0, 0), (1, 0), (3, 0), (0, 1)),
    ((0, 3), (1, 1), (1, 3), (3, 1)),
    ((3, 3), (2, 0), (0, 2)),
    ((3, 2), (2, 3)),
    ((1, 2), (2, 1)),
    ((2, 2),),
)
BACK = (
    (((2, 2), (1, 2)), (), ((0, 2, 2), (1, 2, 2), (0, 1, 2))),
    (((2, 1), (3, 2)), ((1, 2, 1),), ((1, 1, 2), (0, 3, 2), (0, 2, 1), (1, 2, 3))),
    (
        ((2, 3), (2, 0), (0, 2), (1, 1)),
        (),
        ((1, 3, 2), (1, 0, 2), (0, 0, 2), (0, 2, 3), (0, 1, 1), (1, 1, 1), (1, 2, 0)),
    ),
    (
        ((1, 3), (3, 1), (3, 3)),
        ((0, 2, 0),),
        ((0, 1, 3), (1, 3, 1), (0, 3, 1), (1, 1, 3), (0, 3, 3), (1, 3, 3)),
    ),
    (
        ((1, 0), (0, 1), (3, 0), (0, 3)),
        (),
        (
            (1, 0, 1), (1, 0, 3), (0, 0, 1), (0, 0, 3),
            (0, 1, 0), (1, 1, 0), (0, 3, 0), (1, 3, 0),
        ),
    ),
)

FAR_FIRST = sorted(
    [(dx, dy, o) for dx in range(4) for dy in range(4) for o in (0, 1) if dx or dy or o],
    key=lambda d: -min(d[0], 4 - d[0]) - min(d[1], 4 - d[1]),
)


def dot(a, b, dims):
    return lax.dot_general(a, b, dims, preferred_element_type=jnp.float32)


def split3(v):
    hi = v.astype(jnp.bfloat16).astype(jnp.float32)
    rest = v - hi
    mid = rest.astype(jnp.bfloat16).astype(jnp.float32)
    low = rest - mid
    return jnp.concatenate([hi, mid, low], axis=0).astype(jnp.bfloat16)


def kernel(
    hid, ids_t, gain, rout_t, fgain, svec, grades, ranks, wg_hbm, wu_hbm, wd_hbm,
    stat_o, out_o,
    xbuf, wg, wu, wd, gate_s, rinv, toks, gsend, grecv, rk,
    xg, aref, bref, actr, ppart, stage, tsend, trecv, hbuf, headrow, h3, nref, zbuf,
    psend, precv, vq, vf, uq, uf, ggsend, gown, acc,
    wsem, ag_s, ag_r, pt_s, pt_r, small_s, small_r, pr_s, pr_r, tr_s, vq_r, vf_r, uq_r, uf_r, ready,
):
    tokens, width = hid.shape
    units = wg.shape[1]
    half, quarter = tokens // 2, tokens // 4
    planes = zbuf.shape[0]
    me = lax.axis_index("exp")
    z = lax.axis_index("psg")
    core = lax.rem(me, 2)
    cx = lax.rem(lax.div(me, 2), 4)
    cy = lax.div(me, 8)

    def at(dx, dy, other=0):
        side = (1 - core) if other else core
        return (lax.rem(cy + dy, 4) * 4 + lax.rem(cx + dx, 4)) * 2 + side

    barrier = pltpu.get_barrier_semaphore()
    beside = [{"exp": at(*d)} for d in ((1, 0), (3, 0), (0, 1), (0, 3), (0, 0, 1))]
    beside += [{"psg": lax.rem(z + i, planes)} for i in (1, planes - 1)]

    def greet(sem):
        for device in beside:
            pl.semaphore_signal(sem, inc=1, device_id=device, device_id_type=MESH)

    def widen(k):
        greet(ready.at[k])
        pl.semaphore_wait(ready.at[k], len(beside))

    greet(barrier)
    loads = [
        pltpu.make_async_copy(wg_hbm, wg, wsem.at[0]),
        pltpu.make_async_copy(wu_hbm, wu, wsem.at[1]),
        pltpu.make_async_copy(wd_hbm, wd, wsem.at[2]),
    ]
    for load in loads:
        load.start()

    toks[...] = jnp.zeros_like(toks)

    def norm_rows(i, carry):
        rows = pl.ds(pl.multiple_of(i * 16, 16), 16)
        h = hid[rows, :].astype(jnp.float32)
        r = lax.rsqrt(jnp.mean(h * h, axis=1, keepdims=True) + EPS)
        rinv[rows, :] = r
        toks[...] += jnp.sum(h, axis=0, keepdims=True)
        xbuf[me, rows, :] = (h * r * gain[...]).astype(jnp.bfloat16)
        return carry

    lax.fori_loop(0, tokens // 16, norm_rows, 0)
    pl.semaphore_wait(barrier, len(beside))

    pending = []

    def offset(h, du, dv):
        du, dv = du % 4, dv % 4
        return (du, dv) if h == 0 else (dv, du)

    def spot(h, du, dv):
        ox, oy = offset(h, du, dv)
        return oy * 4 + ox

    def rows_of(h, q):
        start = h * half
        if q is None:
            return pl.ds(start, half)
        return pl.ds(start + q * quarter, quarter)

    def send(h, du, dv, q, su, sv):
        block = at(*offset(h, du, dv))
        piece = xbuf.at[block, rows_of(h, q)]
        k = len([1 for kind, _ in pending if kind == 0])
        copy = pltpu.make_async_remote_copy(
            src_ref=piece,
            dst_ref=piece,
            send_sem=ag_s.at[k],
            recv_sem=ag_r.at[h, spot(h, du - su, dv - sv), q or 0],
            device_id={"exp": at(*offset(h, su, sv))},
            device_id_type=MESH,
        )
        copy.start()
        pending.append((0, copy))

    def share(h, du, dv):
        block = at(*offset(h, du, dv))
        piece = xbuf.at[block, rows_of(h, None)]
        k = spot(h, du, dv)
        copy = pltpu.make_async_remote_copy(
            src_ref=piece,
            dst_ref=piece,
            send_sem=pt_s.at[h, k],
            recv_sem=pt_r.at[h, k],
            device_id={"exp": at(0, 0, 1)},
            device_id_type=MESH,
        )
        copy.start()
        pending.append((1, copy))

    def arrive(h, du, dv, q):
        block = at(*offset(h, du, dv))
        piece = xbuf.at[block, rows_of(h, q)]
        pltpu.make_async_copy(piece, piece, ag_r.at[h, spot(h, du, dv), q or 0]).wait()

    for h in (0, 1):
        send(h, 0, 0, None, 1, 0)
        send(h, 0, 0, None, 3, 0)
    for h in (0, 1):
        send(h, 0, 0, None, 0, 1)
        send(h, 0, 0, None, 0, 3)
    for h in (0, 1):
        share(h, 0, 0)

    logits = dot(rout_t[...], xbuf[me], NT)
    experts = lax.broadcasted_iota(jnp.int32, (WAYS, tokens), 0)
    picked = ids_t[0:1, :] == experts
    for k in range(1, ids_t.shape[0]):
        picked = jnp.logical_or(picked, ids_t[k : k + 1, :] == experts)
    weights = jnp.where(picked, jnp.exp(logits), 0.0)
    gates = weights / jnp.sum(weights, axis=0, keepdims=True)
    gate_s[...] = gates
    gate_low = gates.astype(jnp.bfloat16).astype(jnp.float32)
    gsend[:, 0, :] = jnp.where(picked, gate_low, -1.0)
    before = (
        lax.broadcasted_iota(jnp.int32, (tokens, tokens), 0)
        < lax.broadcasted_iota(jnp.int32, (tokens, tokens), 1)
    ).astype(jnp.float32).astype(jnp.bfloat16)

    def rank_of(mask):
        place = dot(mask.astype(jnp.float32).astype(jnp.bfloat16), before, NN)
        return jnp.where(mask, place, -1.0)

    def to_all(source, target, which, put=None):
        for dx, dy, o in FAR_FIRST:
            e = at(dx, dy, o)
            pltpu.make_async_remote_copy(
                src_ref=source(e),
                dst_ref=target.at[me] if put is None else target.at[put],
                send_sem=small_s.at[which],
                recv_sem=small_r.at[which],
                device_id={"exp": e},
                device_id_type=MESH,
            ).start()

    def from_all(target, which, count=WAYS - 1):
        block = target.at[pl.ds(0, count)]
        pltpu.make_async_copy(block, block, small_r.at[which]).wait()

    def sent_all(target, which, count=WAYS - 1):
        block = target.at[pl.ds(0, count)]
        pltpu.make_async_copy(block, block, small_s.at[which]).wait()

    def pair(e):
        return pl.ds(lax.div(e, 2) * 2, 2)

    widen(0)
    widen(1)

    for h in (0, 1):
        arrive(h, 3, 0, None)
        send(h, 3, 0, 0, 1, 0)
        send(h, 3, 0, None, 0, 1)
        send(h, 3, 0, None, 0, 3)
        arrive(h, 1, 0, None)
        send(h, 1, 0, 1, 3, 0)
        send(h, 1, 0, None, 0, 1)
        send(h, 1, 0, None, 0, 3)
    widen(2)
    widen(3)
    to_all(lambda e: gsend.at[pair(e)], grecv, 0, pl.ds(me * 2, 2))
    grecv[pl.ds(me * 2, 2)] = gsend[pair(me)]
    for h in (0, 1):
        arrive(h, 0, 3, None)
        send(h, 0, 3, 0, 0, 1)
        arrive(h, 0, 1, None)
        send(h, 0, 1, 1, 0, 3)
    for h in (0, 1):
        for du, dv in ((3, 0), (1, 0), (0, 3), (0, 1)):
            share(h, du, dv)

    from_all(grecv, 0, 2 * (WAYS - 1))
    everyone = grecv[:, 0, :]
    rk[:, 0, :] = rank_of(everyone >= 0.0)
    for load in loads[:2]:
        load.wait()
    slot = lax.broadcasted_iota(jnp.int32, (SLOTS, tokens), 0).astype(jnp.float32)

    def sources(group, sign=1):
        return [(at((sign * dx) % 4, (sign * dy) % 4, o), dx, dy, o) for dx, dy in group for o in (0, 1)]

    def forward(group):
        for dx, dy in group:
            for h in (0, 1):
                block = at(dx, dy, 1)
                piece = xbuf.at[block, rows_of(h, None)]
                pltpu.make_async_copy(piece, piece, pt_r.at[h, dy * 4 + dx]).wait()
        members = [s for s, _, _, _ in sources(group)]
        rows, gate_col = [], []
        for s in members:
            hit = slot == rk[s * 2 + core]
            one = jnp.where(hit, 1.0, 0.0)
            rows.append(dot(one.astype(jnp.bfloat16), xbuf[s], NN))
            gate_col.append(jnp.sum(jnp.where(hit, grecv[s * 2 + core], 0.0), axis=1, keepdims=True))
        count = len(members) * SLOTS
        xg[0:count, 0:width] = jnp.concatenate(rows, axis=0).astype(jnp.bfloat16)
        weight = jnp.concatenate(gate_col, axis=0)
        step = min(256, units)

        def tile(n, carry):
            cols = pl.ds(pl.multiple_of(n * step, step), step)
            pre_gate = dot(xg[0:count, 0:width], wg[:, cols], NN)
            pre_up = dot(xg[0:count, 0:width], wu[:, cols], NN)
            sig = 1.0 / (1.0 + jnp.exp(-pre_gate))
            silu = pre_gate * sig
            slope = sig * (1.0 + pre_gate * (1.0 - sig))
            act = (silu * pre_up).astype(jnp.bfloat16).astype(jnp.float32)
            to_gate = weight * (pre_up * slope)
            to_up = weight * silu
            part = weight * act
            for i, s in enumerate(members):
                span = slice(i * SLOTS, (i + 1) * SLOTS)
                aref[s, :, cols] = to_gate[span]
                bref[s, :, cols] = to_up[span]
                actr[s, :, cols] = act[span]
                ppart[s, :, cols] = jnp.sum(part[span], axis=0, keepdims=True)
            return carry

        lax.fori_loop(0, units // step, tile, 0)

    forward(GROUPS[0])
    for h in (0, 1):
        for q in (0, 1):
            arrive(h, 2, 0, q)
            send(h, 2, 0, q, 0, 1)
            send(h, 2, 0, q, 0, 3)
        share(h, 2, 0)
    for h in (0, 1):
        for du in (3, 1):
            arrive(h, du, 3, None)
            send(h, du, 3, 0, 0, 1)
            arrive(h, du, 1, None)
            send(h, du, 1, 1, 0, 3)
            share(h, du, 3)
            share(h, du, 1)
    forward(GROUPS[1])
    for h in (0, 1):
        arrive(h, 2, 3, 0)
        send(h, 2, 3, 0, 0, 1)
        arrive(h, 2, 1, 1)
        send(h, 2, 1, 1, 0, 3)
        arrive(h, 2, 3, 1)
        arrive(h, 2, 1, 0)
        share(h, 2, 3)
        share(h, 2, 1)
    for h in (0, 1):
        arrive(h, 0, 2, 0)
        arrive(h, 0, 2, 1)
        share(h, 0, 2)
    forward(GROUPS[2])
    for du, group in ((3, GROUPS[3]), (1, GROUPS[4])):
        for h in (0, 1):
            arrive(h, du, 2, 0)
            arrive(h, du, 2, 1)
            share(h, du, 2)
        forward(group)
    for h in (0, 1):
        arrive(h, 2, 2, 0)
        arrive(h, 2, 2, 1)
        share(h, 2, 2)
    forward(GROUPS[5])

    loads[2].wait()
    xg[0 : 3 * WAYS, 0:units] = split3(ppart[:, 0, :])
    wide = min(256, width)
    lanes = stage.shape[2]
    blocks = width // lanes
    for n in range(width // wide):
        cols = slice(n * wide, (n + 1) * wide)
        t = dot(xg[0 : 3 * WAYS, 0:units], wd[:, cols], NN)
        t = t[0:WAYS] + (t[WAYS : 2 * WAYS] + t[2 * WAYS : 3 * WAYS])
        for j in range(wide // lanes):
            stage[:, n * (wide // lanes) + j, :] = t[:, j * lanes : (j + 1) * lanes]
    tsend[...] = stage[...].astype(jnp.bfloat16)
    to_all(lambda e: tsend.at[e], trecv, 1)
    trecv[me] = tsend[me]
    own = jnp.concatenate(
        [toks[:, j * lanes : (j + 1) * lanes] for j in range(blocks)], axis=0
    )
    head_dir = fgain[...] * svec[...].astype(jnp.float32)
    from_all(trecv, 1)
    pooled = (own + jnp.sum(trecv[...].astype(jnp.float32), axis=0)) / tokens

    def total(v):
        return jnp.sum(jnp.sum(v, axis=1, keepdims=True), axis=0, keepdims=True)

    inv = lax.rsqrt(total(pooled * pooled) / width + EPS)
    score = total(pooled * inv * head_dir)
    lean = total(pooled * head_dir) / width
    head = inv * head_dir - pooled * (inv * inv * inv * lean)
    hbuf[me] = head.astype(jnp.bfloat16)
    zbuf[z] = jnp.broadcast_to(score, (1, zbuf.shape[2]))
    to_all(lambda e: hbuf.at[me], hbuf, 2)
    for i in range(1, planes):
        pltpu.make_async_remote_copy(
            src_ref=zbuf.at[z],
            dst_ref=zbuf.at[z],
            send_sem=small_s.at[3],
            recv_sem=small_r.at[3],
            device_id={"psg": lax.rem(z + i, planes)},
            device_id_type=MESH,
        ).start()
    for j in range(blocks):
        headrow[:, j * lanes : (j + 1) * lanes] = head[j : j + 1]
    from_all(hbuf, 2)
    stage[...] = hbuf[...].astype(jnp.float32)
    for j in range(blocks):
        h3[:, j * lanes : (j + 1) * lanes] = stage[:, j, :].astype(jnp.bfloat16)
    step = min(256, units)

    def near_tile(n, carry):
        cols = pl.ds(pl.multiple_of(n * step, step), step)
        nref[:, 0, cols] = dot(h3[...], wd[cols, :], NT)
        return carry

    lax.fori_loop(0, units // step, near_tile, 0)

    for _, copy in pending:
        copy.wait_send()
    back = []
    turns = width // wide // 2

    def backward(group):
        members = sources(group)
        count = len(members) * SLOTS
        xg[0:count, 0:units] = jnp.concatenate(
            [aref[s] * nref[s] for s, _, _, _ in members], axis=0
        ).astype(jnp.bfloat16)
        xg[0:count, units : 2 * units] = jnp.concatenate(
            [bref[s] * nref[s] for s, _, _, _ in members], axis=0
        ).astype(jnp.bfloat16)

        def tile(n, carry):
            cols = pl.ds(pl.multiple_of(n * wide, wide), wide)
            g = dot(xg[0:count, 0:units], wg[cols, :], NT)
            g = g + dot(xg[0:count, units : 2 * units], wu[cols, :], NT)
            for i, (s, dx, dy, o) in enumerate(members):
                mine = g[i * SLOTS : (i + 1) * SLOTS].astype(jnp.bfloat16)
                if o:
                    psend[dy * 4 + dx, :, cols] = mine
                else:
                    xbuf[16 + dy * 4 + dx, 0:SLOTS, cols] = mine
            return carry

        for c in (0, 1):
            lax.fori_loop(c * turns, (c + 1) * turns, tile, 0)
            for dx, dy in group:
                k = dy * 4 + dx
                cols = pl.ds(c * (width // 2), width // 2)
                copy = pltpu.make_async_remote_copy(
                    src_ref=psend.at[k, :, cols],
                    dst_ref=precv.at[k, :, cols],
                    send_sem=pr_s.at[c, k],
                    recv_sem=pr_r.at[c, k],
                    device_id={"exp": at(0, 0, 1)},
                    device_id_type=MESH,
                )
                copy.start()
                back.append(copy)

    def gather(group):
        hits = []
        for dx, dy in group:
            s = at(dx, dy)
            for r in (s * 2 + core, s * 2 + 1 - core):
                hits.append(jnp.where(slot == rk[r], 1.0, 0.0).T.astype(jnp.bfloat16))
        def tile(n, carry):
            cols = pl.ds(pl.multiple_of(n * wide, wide), wide)
            for i, (dx, dy) in enumerate(group):
                k = dy * 4 + dx
                rows = dot(hits[2 * i], xbuf[16 + k, 0:SLOTS, cols], NN)
                rows = rows + dot(hits[2 * i + 1], precv[k, :, cols], NN)
                xbuf[k, :, cols] = rows.astype(jnp.bfloat16)
            return carry

        for c in (0, 1):
            for dx, dy in group:
                k = dy * 4 + dx
                piece = precv.at[k, :, pl.ds(c * (width // 2), width // 2)]
                pltpu.make_async_copy(piece, piece, pr_r.at[c, k]).wait()
            lax.fori_loop(c * turns, (c + 1) * turns, tile, 0)

    def hand(h, k, q, to, landing, sem):
        copy = pltpu.make_async_remote_copy(
            src_ref=xbuf.at[k, rows_of(h, q)],
            dst_ref=landing,
            send_sem=tr_s.at[len(hops)],
            recv_sem=sem,
            device_id={"exp": to},
            device_id_type=MESH,
        )
        copy.start()
        hops.append(copy)

    hops = []

    def landed(ref, sem):
        pltpu.make_async_copy(ref, ref, sem).wait()

    def add(h, k, q, refs):
        start = h * half + (q or 0) * quarter
        count = half if q is None else quarter

        def rows16(i, carry):
            here = pl.ds(pl.multiple_of(start + i * 16, 16), 16)
            there = pl.ds(pl.multiple_of(i * 16, 16), 16)
            total = xbuf[k, here, :].astype(jnp.float32)
            for ref in refs:
                total = total + ref[there, :].astype(jnp.float32)
            xbuf[k, here, :] = total.astype(jnp.bfloat16)
            return carry

        lax.fori_loop(0, count // 16, rows16, 0)

    def relay(h, du, dv):
        k = spot(h, du, dv)
        if dv == 2:
            hand(h, k, 0, at(*offset(h, 0, 1)), vq.at[h, du, 0], vq_r.at[h, du, 0])
            hand(h, k, 1, at(*offset(h, 0, 3)), vq.at[h, du, 1], vq_r.at[h, du, 1])
            return
        if dv in (1, 3):
            side = 0 if dv == 1 else 1
            landed(vq.at[h, du, side], vq_r.at[h, du, side])
            add(h, k, side, [vq.at[h, du, side]])
            hand(h, k, None, at(*offset(h, 0, dv)), vf.at[h, du, side], vf_r.at[h, du, side])
            return
        for side in (0, 1):
            landed(vf.at[h, du, side], vf_r.at[h, du, side])
        if du == 0:
            for side in (0, 1):
                landed(uf.at[h, side], uf_r.at[h, side])

            def last(i, carry):
                here = pl.ds(pl.multiple_of(h * half + i * 16, 16), 16)
                there = pl.ds(pl.multiple_of(i * 16, 16), 16)
                total = acc[here, :] + xbuf[k, here, :].astype(jnp.float32)
                for side in (0, 1):
                    total = total + vf[h, du, side, there, :].astype(jnp.float32)
                    total = total + uf[h, side, there, :].astype(jnp.float32)
                acc[here, :] = total
                return carry

            lax.fori_loop(0, half // 16, last, 0)
            return
        add(h, k, None, [vf.at[h, du, 0], vf.at[h, du, 1]])
        if du == 2:
            hand(h, k, 0, at(*offset(h, 1, 0)), uq.at[h, 0], uq_r.at[h, 0])
            hand(h, k, 1, at(*offset(h, 3, 0)), uq.at[h, 1], uq_r.at[h, 1])
            return
        side = 0 if du == 1 else 1
        landed(uq.at[h, side], uq_r.at[h, side])
        add(h, k, side, [uq.at[h, side]])
        hand(h, k, None, at(*offset(h, du, 0)), uf.at[h, side], uf_r.at[h, side])

    for group, early, late in BACK:
        backward(group)
        for step_of in early:
            relay(*step_of)
        gather(group)
        for step_of in late:
            relay(*step_of)

    def gate_gradient(s, carry):
        gg = jnp.sum(actr[s] * nref[s], axis=1, keepdims=True)
        ggsend[s] = jnp.sum(
            jnp.where(slot == rk[s * 2 + core], gg, 0.0), axis=0, keepdims=True
        )
        return carry

    lax.fori_loop(0, WAYS, gate_gradient, 0)
    to_all(lambda e: ggsend.at[e], gown, 4)
    gown[me] = ggsend[me]
    backward(((0, 0),))
    gather(((0, 0),))

    from_all(zbuf, 3, planes - 1)
    eye_r = lax.broadcasted_iota(jnp.int32, (planes, planes), 0)
    eye_c = lax.broadcasted_iota(jnp.int32, (planes, planes), 1)
    eye = eye_r == eye_c

    def column(row):
        return jnp.sum(jnp.where(eye, row, 0.0), axis=1, keepdims=True)

    g_row = grades[...].astype(jnp.float32)
    g_col = column(g_row)
    s_col = zbuf[:, 0, 0:1]
    s_row = jnp.sum(jnp.where(eye, s_col, 0.0), axis=0, keepdims=True)
    ln2 = 0.6931471805599453
    d_row = ln2 / jnp.log(2.0 + ranks[...].astype(jnp.float32))
    d_col = column(d_row)
    worth_row = jnp.exp2(g_row)
    worth_col = column(worth_row)
    ahead = jnp.logical_or(g_row > g_col, jnp.logical_and(g_row == g_col, eye_c < eye_r))
    ideal = jnp.sum(jnp.where(ahead, 1.0, 0.0), axis=1, keepdims=True)
    ideal_gain = jnp.sum((worth_col - 1.0) * ln2 / jnp.log(2.0 + ideal), axis=0, keepdims=True)
    swap = jnp.abs((worth_col - worth_row) * (d_col - d_row)) / ideal_gain
    swap = jnp.where(g_col > g_row, swap, 0.0)
    margin = s_col - s_row
    soft = jnp.maximum(-margin, 0.0) + jnp.log(1.0 + jnp.exp(-jnp.abs(margin)))
    loss = total(swap * soft)
    pull = swap / (1.0 + jnp.exp(margin))
    d_own = jnp.sum(jnp.where(eye_c == z, pull, 0.0) - jnp.where(eye_r == z, pull, 0.0))
    spot_of = lax.broadcasted_iota(jnp.int32, stat_o.shape, 1)
    stat_o[...] = jnp.where(spot_of == 0, loss, score)
    scale = d_own * (LOSS_SCALE / tokens)

    from_all(gown, 4)
    gate_grad = gown[:, 0, :]
    gates = gate_s[...]
    d_logit = gates * (gate_grad - jnp.sum(gates * gate_grad, axis=0, keepdims=True))
    d_logit = split3(d_logit)
    rout3 = jnp.concatenate([rout_t[...]] * 3, axis=0)
    acc[...] = dot(d_logit, rout3, TN)
    head = headrow[...]

    def finish(i, carry):
        rows = pl.ds(pl.multiple_of(i * 16, 16), 16)
        h = hid[rows, :].astype(jnp.float32)
        r = rinv[rows, :]
        scaled = acc[rows, :] * gain[...]
        lean = jnp.mean(h * scaled, axis=1, keepdims=True)
        full = r * scaled - h * (r * r * r * lean) + head
        out_o[rows, :] = (full * scale).astype(jnp.bfloat16)
        return carry

    for h in (0, 1):
        relay(h, 0, 0)
        lax.fori_loop(h * half // 16, (h + 1) * half // 16, finish, 0)
    for copy in back + hops:
        copy.wait_send()
    sent_all(grecv, 0, 2 * (WAYS - 1))
    sent_all(tsend, 1)
    sent_all(hbuf, 2)
    sent_all(zbuf, 3, planes - 1)
    sent_all(gown, 4)


def local(
    hidden,
    norm_gain,
    router,
    gate_proj,
    up_proj,
    down_proj,
    final_gain,
    score_vector,
    expert_ids,
    grades,
    passage_ranks,
):
    tokens, width = hidden.shape[2:]
    units = gate_proj.shape[2]
    planes = lax.axis_size("psg")
    f32, bf16 = jnp.float32, jnp.bfloat16
    vmem = pl.BlockSpec(memory_space=pltpu.VMEM)
    any_space = pl.BlockSpec(memory_space=pl.ANY)
    scratch = [
        pltpu.VMEM((WAYS, tokens, width), bf16),
        pltpu.VMEM((width, units), bf16),
        pltpu.VMEM((width, units), bf16),
        pltpu.VMEM((units, width), bf16),
        pltpu.VMEM((WAYS, tokens), f32),
        pltpu.VMEM((tokens, 1), f32),
        pltpu.VMEM((1, width), f32),
        pltpu.VMEM((WAYS, 1, tokens), f32),
        pltpu.VMEM((2 * WAYS, 1, tokens), f32),
        pltpu.VMEM((2 * WAYS, 1, tokens), f32),
        pltpu.VMEM((8 * SLOTS, max(width, 2 * units)), bf16),
        pltpu.VMEM((WAYS, SLOTS, units), f32),
        pltpu.VMEM((WAYS, SLOTS, units), f32),
        pltpu.VMEM((WAYS, SLOTS, units), f32),
        pltpu.VMEM((WAYS, 1, units), f32),
        pltpu.VMEM((WAYS, width // 128, 128), f32),
        pltpu.VMEM((WAYS, width // 128, 128), bf16),
        pltpu.VMEM((WAYS, width // 128, 128), bf16),
        pltpu.VMEM((WAYS, width // 128, 128), bf16),
        pltpu.VMEM((1, width), f32),
        pltpu.VMEM((WAYS, width), bf16),
        pltpu.VMEM((WAYS, 1, units), f32),
        pltpu.VMEM((planes, 1, tokens), f32),
        pltpu.VMEM((16, SLOTS, width), bf16),
        pltpu.VMEM((16, SLOTS, width), bf16),
        pltpu.VMEM((2, 4, 2, tokens // 4, width), bf16),
        pltpu.VMEM((2, 4, 2, tokens // 2, width), bf16),
        pltpu.VMEM((2, 2, tokens // 4, width), bf16),
        pltpu.VMEM((2, 2, tokens // 2, width), bf16),
        pltpu.VMEM((WAYS, 1, tokens), f32),
        pltpu.VMEM((WAYS, 1, tokens), f32),
        pltpu.VMEM((tokens, width), f32),
        pltpu.SemaphoreType.DMA((3,)),
        pltpu.SemaphoreType.DMA((44,)),
        pltpu.SemaphoreType.DMA((2, 16, 2)),
        pltpu.SemaphoreType.DMA((2, 16)),
        pltpu.SemaphoreType.DMA((2, 16)),
        pltpu.SemaphoreType.DMA((5,)),
        pltpu.SemaphoreType.DMA((5,)),
        pltpu.SemaphoreType.DMA((2, 16)),
        pltpu.SemaphoreType.DMA((2, 16)),
        pltpu.SemaphoreType.DMA((40,)),
        pltpu.SemaphoreType.DMA((2, 4, 2)),
        pltpu.SemaphoreType.DMA((2, 4, 2)),
        pltpu.SemaphoreType.DMA((2, 2)),
        pltpu.SemaphoreType.DMA((2, 2)),
        pltpu.SemaphoreType.REGULAR((4,)),
    ]
    stat, grad = pl.pallas_call(
        kernel,
        out_shape=(
            jax.ShapeDtypeStruct((1, 128), f32),
            jax.ShapeDtypeStruct((tokens, width), bf16),
        ),
        in_specs=[vmem] * 8 + [any_space] * 3,
        out_specs=(vmem, vmem),
        scratch_shapes=scratch,
        compiler_params=pltpu.CompilerParams(
            collective_id=0, has_side_effects=True, vmem_limit_bytes=62 * 1024 * 1024
        ),
        name="expert_block",
    )(
        hidden.reshape(tokens, width),
        expert_ids.reshape(tokens, -1).T,
        norm_gain.reshape(1, width),
        router.T,
        final_gain.reshape(width // 128, 128),
        score_vector.reshape(width // 128, 128),
        grades,
        passage_ranks,
        gate_proj[0],
        up_proj[0],
        down_proj[0],
    )
    return stat[0, 0:1], stat[0:1, 1:2], grad.reshape(1, 1, tokens, width)


def solution(mesh):
    placed = (
        P("exp", "psg", None, None),
        P(),
        P(),
        P("exp", None, None),
        P("exp", None, None),
        P("exp", None, None),
        P(),
        P(),
        P("exp", "psg", None, None),
        P("exp", None),
        P("exp", None),
    )
    return jax.shard_map(
        local,
        mesh=mesh,
        in_specs=placed,
        out_specs=(P("exp"), P("exp", "psg"), P("exp", "psg", None, None)),
        check_vma=False,
    )
```

```python
import jax
import jax.numpy as jnp
from jax import lax
from jax.experimental import pallas as pl
from jax.experimental.pallas import tpu as pltpu
from jax.sharding import PartitionSpec as P

MESH = pl.DeviceIdType.MESH
EPS = 1e-06
LOSS_SCALE = 256.0
SLOTS = 40
WAYS = 32
NN = (((1,), (0,)), ((), ()))
NT = (((1,), (1,)), ((), ()))
TN = (((0,), (0,)), ((), ()))

GROUPS = (
    ((0, 0), (1, 0), (3, 0), (0, 1)),
    ((0, 3), (1, 1), (1, 3), (3, 1)),
    ((3, 3), (2, 0), (0, 2)),
    ((3, 2), (2, 3)),
    ((1, 2), (2, 1)),
    ((2, 2),),
)
BACK = (
    (
        ((2, 2), (1, 2)),
        (),
        ((0, 2, 2), (1, 2, 2), (0, 1, 2)),
    ),
    (
        ((2, 1), (3, 2)),
        (),
        ((1, 1, 2), (0, 3, 2)),
    ),
    (
        ((2, 3), (2, 0), (0, 2), (1, 1)),
        ((1, 2, 1), (0, 2, 1), (1, 2, 3)),
        ((1, 3, 2), (1, 0, 2), (0, 0, 2), (0, 2, 3)),
    ),
    (
        ((1, 3), (3, 1), (3, 3)),
        ((0, 1, 1), (1, 1, 1), (1, 2, 0)),
        ((0, 2, 0), (0, 1, 3), (1, 1, 3), (0, 3, 1), (0, 3, 3)),
    ),
    (
        ((1, 0), (0, 1), (3, 0), (0, 3)),
        ((1, 3, 1), (1, 3, 3)),
        ((1, 0, 1), (1, 0, 3), (0, 0, 1), (0, 0, 3), (0, 1, 0), (1, 1, 0), (0, 3, 0), (1, 3, 0)),
    ),
)
FAR_FIRST = sorted(
    [(dx, dy, o) for dx in range(4) for dy in range(4) for o in (0, 1) if dx or dy or o],
    key=lambda d: -min(d[0], 4 - d[0]) - min(d[1], 4 - d[1]),
)


def dot(a, b, dims):
    return lax.dot_general(a, b, dims, preferred_element_type=jnp.float32)


def split3(v):
    hi = v.astype(jnp.bfloat16).astype(jnp.float32)
    rest = v - hi
    mid = rest.astype(jnp.bfloat16).astype(jnp.float32)
    low = rest - mid
    return jnp.concatenate([hi, mid, low], axis=0).astype(jnp.bfloat16)


def kernel(
    hid, ids_t, gain, rout_t, fgain, svec, grades, ranks, wg_hbm, wu_hbm, wd_hbm,
    stat_o, out_o,
    xbuf, wg, wu, wd, gate_s, rinv, toks, gsend, grecv, rk,
    xg, aref, bref, actr, ppart, stage, tsend, trecv, hbuf, headrow, h3, nref, zbuf,
    psend, precv, vq, vf, uq, uf, ggsend, gown, acc,
    wsem, ag_s, ag_r, pt_s, pt_r, small_s, small_r, pr_s, pr_r, tr_s, vq_r, vf_r, uq_r, uf_r, ready,
):
    tokens, width = hid.shape
    units = wg.shape[1]
    half, quarter = tokens // 2, tokens // 4
    planes = zbuf.shape[0]
    me = lax.axis_index("exp")
    z = lax.axis_index("psg")
    core = lax.rem(me, 2)
    cx = lax.rem(lax.div(me, 2), 4)
    cy = lax.div(me, 8)

    def at(dx, dy, other=0):
        side = (1 - core) if other else core
        return (lax.rem(cy + dy, 4) * 4 + lax.rem(cx + dx, 4)) * 2 + side

    barrier = pltpu.get_barrier_semaphore()
    beside = [{"exp": at(*d)} for d in ((1, 0), (3, 0), (0, 1), (0, 3), (0, 0, 1))]
    beside += [{"psg": lax.rem(z + i, planes)} for i in (1, planes - 1)]

    def greet(sem):
        for device in beside:
            pl.semaphore_signal(sem, inc=1, device_id=device, device_id_type=MESH)

    def widen(k):
        greet(ready.at[k])
        pl.semaphore_wait(ready.at[k], len(beside))

    greet(barrier)
    loads = [
        pltpu.make_async_copy(wg_hbm, wg, wsem.at[0]),
        pltpu.make_async_copy(wu_hbm, wu, wsem.at[1]),
        pltpu.make_async_copy(wd_hbm, wd, wsem.at[2]),
    ]
    for load in loads:
        load.start()

    toks[...] = jnp.zeros_like(toks)

    def norm_rows(i, carry):
        rows = pl.ds(pl.multiple_of(i * 16, 16), 16)
        h = hid[rows, :].astype(jnp.float32)
        r = lax.rsqrt(jnp.mean(h * h, axis=1, keepdims=True) + EPS)
        rinv[rows, :] = r
        toks[...] += jnp.sum(h, axis=0, keepdims=True)
        xbuf[me, rows, :] = (h * r * gain[...]).astype(jnp.bfloat16)
        return carry

    lax.fori_loop(0, tokens // 16, norm_rows, 0)

    logits = dot(rout_t[...], xbuf[me], NT)
    experts = lax.broadcasted_iota(jnp.int32, (WAYS, tokens), 0)
    picked = ids_t[0:1, :] == experts
    for k in range(1, ids_t.shape[0]):
        picked = jnp.logical_or(picked, ids_t[k : k + 1, :] == experts)
    weights = jnp.where(picked, jnp.exp(logits), 0.0)
    gates = weights / jnp.sum(weights, axis=0, keepdims=True)
    gate_s[...] = gates
    gate_low = gates.astype(jnp.bfloat16).astype(jnp.float32)
    gsend[:, 0, :] = jnp.where(picked, gate_low, -1.0)
    before = (
        lax.broadcasted_iota(jnp.int32, (tokens, tokens), 0)
        < lax.broadcasted_iota(jnp.int32, (tokens, tokens), 1)
    ).astype(jnp.float32).astype(jnp.bfloat16)

    def rank_of(mask):
        place = dot(mask.astype(jnp.float32).astype(jnp.bfloat16), before, NN)
        return jnp.where(mask, place, -1.0)

    pl.semaphore_wait(barrier, len(beside))

    pending = []

    def offset(h, du, dv):
        du, dv = du % 4, dv % 4
        return (du, dv) if h == 0 else (dv, du)

    def spot(h, du, dv):
        ox, oy = offset(h, du, dv)
        return oy * 4 + ox

    def rows_of(h, q):
        start = h * half
        if q is None:
            return pl.ds(start, half)
        return pl.ds(start + q * quarter, quarter)

    def send(h, du, dv, q, su, sv):
        block = at(*offset(h, du, dv))
        piece = xbuf.at[block, rows_of(h, q)]
        k = len([1 for kind, _ in pending if kind == 0])
        copy = pltpu.make_async_remote_copy(
            src_ref=piece,
            dst_ref=piece,
            send_sem=ag_s.at[k],
            recv_sem=ag_r.at[h, spot(h, du - su, dv - sv), q or 0],
            device_id={"exp": at(*offset(h, su, sv))},
            device_id_type=MESH,
        )
        copy.start()
        pending.append((0, copy))

    def share(h, du, dv):
        block = at(*offset(h, du, dv))
        piece = xbuf.at[block, rows_of(h, None)]
        k = spot(h, du, dv)
        copy = pltpu.make_async_remote_copy(
            src_ref=piece,
            dst_ref=piece,
            send_sem=pt_s.at[h, k],
            recv_sem=pt_r.at[h, k],
            device_id={"exp": at(0, 0, 1)},
            device_id_type=MESH,
        )
        copy.start()
        pending.append((1, copy))

    def arrive(h, du, dv, q):
        block = at(*offset(h, du, dv))
        piece = xbuf.at[block, rows_of(h, q)]
        pltpu.make_async_copy(piece, piece, ag_r.at[h, spot(h, du, dv), q or 0]).wait()

    for h in (0, 1):
        send(h, 0, 0, None, 1, 0)
        send(h, 0, 0, None, 3, 0)

    def to_all(source, target, which, put=None):
        for dx, dy, o in FAR_FIRST:
            e = at(dx, dy, o)
            pltpu.make_async_remote_copy(
                src_ref=source(e),
                dst_ref=target.at[me] if put is None else target.at[put],
                send_sem=small_s.at[which],
                recv_sem=small_r.at[which],
                device_id={"exp": e},
                device_id_type=MESH,
            ).start()

    def from_all(target, which, count=WAYS - 1):
        block = target.at[pl.ds(0, count)]
        pltpu.make_async_copy(block, block, small_r.at[which]).wait()

    def sent_all(target, which, count=WAYS - 1):
        block = target.at[pl.ds(0, count)]
        pltpu.make_async_copy(block, block, small_s.at[which]).wait()

    def pair(e):
        return pl.ds(lax.div(e, 2) * 2, 2)

    for k in range(4):
        widen(k)
    to_all(lambda e: gsend.at[pair(e)], grecv, 0, pl.ds(me * 2, 2))
    grecv[pl.ds(me * 2, 2)] = gsend[pair(me)]
    for h in (0, 1):
        send(h, 0, 0, None, 0, 1)
        send(h, 0, 0, None, 0, 3)
    for h in (0, 1):
        share(h, 0, 0)

    for h in (0, 1):
        arrive(h, 3, 0, None)
        send(h, 3, 0, 0, 1, 0)
        send(h, 3, 0, None, 0, 1)
        send(h, 3, 0, None, 0, 3)
        arrive(h, 1, 0, None)
        send(h, 1, 0, 1, 3, 0)
        send(h, 1, 0, None, 0, 1)
        send(h, 1, 0, None, 0, 3)
    for h in (0, 1):
        arrive(h, 0, 3, None)
        send(h, 0, 3, 0, 0, 1)
        arrive(h, 0, 1, None)
        send(h, 0, 1, 1, 0, 3)
    for h in (0, 1):
        for du, dv in ((3, 0), (1, 0), (0, 3), (0, 1)):
            share(h, du, dv)

    from_all(grecv, 0, 2 * (WAYS - 1))
    everyone = grecv[:, 0, :]
    rk[:, 0, :] = rank_of(everyone >= 0.0)
    for load in loads[:2]:
        load.wait()
    slot = lax.broadcasted_iota(jnp.int32, (SLOTS, tokens), 0).astype(jnp.float32)

    def sources(group, sign=1):
        return [(at((sign * dx) % 4, (sign * dy) % 4, o), dx, dy, o) for dx, dy in group for o in (0, 1)]

    def forward(group):
        for dx, dy in group:
            for h in (0, 1):
                block = at(dx, dy, 1)
                piece = xbuf.at[block, rows_of(h, None)]
                pltpu.make_async_copy(piece, piece, pt_r.at[h, dy * 4 + dx]).wait()
        members = [s for s, _, _, _ in sources(group)]
        rows, gate_col = [], []
        for s in members:
            hit = slot == rk[s * 2 + core]
            one = jnp.where(hit, 1.0, 0.0)
            rows.append(dot(one.astype(jnp.bfloat16), xbuf[s], NN))
            gate_col.append(jnp.sum(jnp.where(hit, grecv[s * 2 + core], 0.0), axis=1, keepdims=True))
        count = len(members) * SLOTS
        xg[0:count, 0:width] = jnp.concatenate(rows, axis=0).astype(jnp.bfloat16)
        weight = jnp.concatenate(gate_col, axis=0)
        step = min(256, units)

        def tile(n, carry):
            cols = pl.ds(pl.multiple_of(n * step, step), step)
            pre_gate = dot(xg[0:count, 0:width], wg[:, cols], NN)
            pre_up = dot(xg[0:count, 0:width], wu[:, cols], NN)
            sig = 1.0 / (1.0 + jnp.exp(-pre_gate))
            silu = pre_gate * sig
            slope = sig * (1.0 + pre_gate * (1.0 - sig))
            act = (silu * pre_up).astype(jnp.bfloat16).astype(jnp.float32)
            to_gate = weight * (pre_up * slope)
            to_up = weight * silu
            part = weight * act
            for i, s in enumerate(members):
                span = slice(i * SLOTS, (i + 1) * SLOTS)
                aref[s, :, cols] = to_gate[span]
                bref[s, :, cols] = to_up[span]
                actr[s, :, cols] = act[span]
                ppart[s, :, cols] = jnp.sum(part[span], axis=0, keepdims=True)
            return carry

        lax.fori_loop(0, units // step, tile, 0)

    forward(GROUPS[0])
    for h in (0, 1):
        for q in (0, 1):
            arrive(h, 2, 0, q)
            send(h, 2, 0, q, 0, 1)
            send(h, 2, 0, q, 0, 3)
        share(h, 2, 0)
    for h in (0, 1):
        for du in (3, 1):
            arrive(h, du, 3, None)
            send(h, du, 3, 0, 0, 1)
            arrive(h, du, 1, None)
            send(h, du, 1, 1, 0, 3)
            share(h, du, 3)
            share(h, du, 1)
    forward(GROUPS[1])
    for h in (0, 1):
        arrive(h, 2, 3, 0)
        send(h, 2, 3, 0, 0, 1)
        arrive(h, 2, 1, 1)
        send(h, 2, 1, 1, 0, 3)
        arrive(h, 2, 3, 1)
        arrive(h, 2, 1, 0)
        share(h, 2, 3)
        share(h, 2, 1)
    for h in (0, 1):
        arrive(h, 0, 2, 0)
        arrive(h, 0, 2, 1)
        share(h, 0, 2)
    forward(GROUPS[2])
    for du, group in ((3, GROUPS[3]), (1, GROUPS[4])):
        for h in (0, 1):
            arrive(h, du, 2, 0)
            arrive(h, du, 2, 1)
            share(h, du, 2)
        forward(group)
    for h in (0, 1):
        arrive(h, 2, 2, 0)
        arrive(h, 2, 2, 1)
        share(h, 2, 2)
    forward(GROUPS[5])

    loads[2].wait()
    xg[0 : 3 * WAYS, 0:units] = split3(ppart[:, 0, :])
    wide = min(256, width)
    lanes = stage.shape[2]
    blocks = width // lanes
    for n in range(width // wide):
        cols = slice(n * wide, (n + 1) * wide)
        t = dot(xg[0 : 3 * WAYS, 0:units], wd[:, cols], NN)
        t = t[0:WAYS] + (t[WAYS : 2 * WAYS] + t[2 * WAYS : 3 * WAYS])
        for j in range(wide // lanes):
            stage[:, n * (wide // lanes) + j, :] = t[:, j * lanes : (j + 1) * lanes]
    tsend[...] = stage[...].astype(jnp.bfloat16)
    to_all(lambda e: tsend.at[e], trecv, 1)
    trecv[me] = tsend[me]
    own = jnp.concatenate(
        [toks[:, j * lanes : (j + 1) * lanes] for j in range(blocks)], axis=0
    )
    head_dir = fgain[...] * svec[...].astype(jnp.float32)
    from_all(trecv, 1)
    pooled = (own + jnp.sum(trecv[...].astype(jnp.float32), axis=0)) / tokens

    def total(v):
        return jnp.sum(jnp.sum(v, axis=1, keepdims=True), axis=0, keepdims=True)

    inv = lax.rsqrt(total(pooled * pooled) / width + EPS)
    score = total(pooled * inv * head_dir)
    lean = total(pooled * head_dir) / width
    head = inv * head_dir - pooled * (inv * inv * inv * lean)
    hbuf[me] = head.astype(jnp.bfloat16)
    zbuf[z] = jnp.broadcast_to(score, (1, zbuf.shape[2]))
    to_all(lambda e: hbuf.at[me], hbuf, 2)
    for i in range(1, planes):
        pltpu.make_async_remote_copy(
            src_ref=zbuf.at[z],
            dst_ref=zbuf.at[z],
            send_sem=small_s.at[3],
            recv_sem=small_r.at[3],
            device_id={"psg": lax.rem(z + i, planes)},
            device_id_type=MESH,
        ).start()
    for j in range(blocks):
        headrow[:, j * lanes : (j + 1) * lanes] = head[j : j + 1]
    from_all(hbuf, 2)
    stage[...] = hbuf[...].astype(jnp.float32)
    for j in range(blocks):
        h3[:, j * lanes : (j + 1) * lanes] = stage[:, j, :].astype(jnp.bfloat16)
    step = min(256, units)

    def near_tile(n, carry):
        cols = pl.ds(pl.multiple_of(n * step, step), step)
        nref[:, 0, cols] = dot(h3[...], wd[cols, :], NT)
        return carry

    lax.fori_loop(0, units // step, near_tile, 0)

    for _, copy in pending:
        copy.wait_send()
    back = []
    turns = width // wide // 2

    def backward(group):
        members = sources(group)
        count = len(members) * SLOTS
        xg[0:count, 0:units] = jnp.concatenate(
            [aref[s] * nref[s] for s, _, _, _ in members], axis=0
        ).astype(jnp.bfloat16)
        xg[0:count, units : 2 * units] = jnp.concatenate(
            [bref[s] * nref[s] for s, _, _, _ in members], axis=0
        ).astype(jnp.bfloat16)

        def tile(n, carry):
            cols = pl.ds(pl.multiple_of(n * wide, wide), wide)
            g = dot(xg[0:count, 0:units], wg[cols, :], NT)
            g = g + dot(xg[0:count, units : 2 * units], wu[cols, :], NT)
            for i, (s, dx, dy, o) in enumerate(members):
                mine = g[i * SLOTS : (i + 1) * SLOTS].astype(jnp.bfloat16)
                if o:
                    psend[dy * 4 + dx, :, cols] = mine
                else:
                    xbuf[16 + dy * 4 + dx, 0:SLOTS, cols] = mine
            return carry

        for c in (0, 1):
            lax.fori_loop(c * turns, (c + 1) * turns, tile, 0)
            for dx, dy in group:
                k = dy * 4 + dx
                cols = pl.ds(c * (width // 2), width // 2)
                copy = pltpu.make_async_remote_copy(
                    src_ref=psend.at[k, :, cols],
                    dst_ref=precv.at[k, :, cols],
                    send_sem=pr_s.at[c, k],
                    recv_sem=pr_r.at[c, k],
                    device_id={"exp": at(0, 0, 1)},
                    device_id_type=MESH,
                )
                copy.start()
                back.append(copy)

    def gather(group):
        hits = []
        for dx, dy in group:
            s = at(dx, dy)
            for r in (s * 2 + core, s * 2 + 1 - core):
                hits.append(jnp.where(slot == rk[r], 1.0, 0.0).T.astype(jnp.bfloat16))
        def tile(n, carry):
            cols = pl.ds(pl.multiple_of(n * wide, wide), wide)
            for i, (dx, dy) in enumerate(group):
                k = dy * 4 + dx
                rows = dot(hits[2 * i], xbuf[16 + k, 0:SLOTS, cols], NN)
                rows = rows + dot(hits[2 * i + 1], precv[k, :, cols], NN)
                xbuf[k, :, cols] = rows.astype(jnp.bfloat16)
            return carry

        for c in (0, 1):
            for dx, dy in group:
                k = dy * 4 + dx
                piece = precv.at[k, :, pl.ds(c * (width // 2), width // 2)]
                pltpu.make_async_copy(piece, piece, pr_r.at[c, k]).wait()
            lax.fori_loop(c * turns, (c + 1) * turns, tile, 0)

    def hand(h, k, q, to, landing, sem):
        copy = pltpu.make_async_remote_copy(
            src_ref=xbuf.at[k, rows_of(h, q)],
            dst_ref=landing,
            send_sem=tr_s.at[len(hops)],
            recv_sem=sem,
            device_id={"exp": to},
            device_id_type=MESH,
        )
        copy.start()
        hops.append(copy)

    hops = []

    def landed(ref, sem):
        pltpu.make_async_copy(ref, ref, sem).wait()

    def add(h, k, q, refs):
        start = h * half + (q or 0) * quarter
        count = half if q is None else quarter

        def rows16(i, carry):
            here = pl.ds(pl.multiple_of(start + i * 16, 16), 16)
            there = pl.ds(pl.multiple_of(i * 16, 16), 16)
            total = xbuf[k, here, :].astype(jnp.float32)
            for ref in refs:
                total = total + ref[there, :].astype(jnp.float32)
            xbuf[k, here, :] = total.astype(jnp.bfloat16)
            return carry

        lax.fori_loop(0, count // 16, rows16, 0)

    def relay(h, du, dv):
        k = spot(h, du, dv)
        if dv == 2:
            hand(h, k, 0, at(*offset(h, 0, 1)), vq.at[h, du, 0], vq_r.at[h, du, 0])
            hand(h, k, 1, at(*offset(h, 0, 3)), vq.at[h, du, 1], vq_r.at[h, du, 1])
            return
        if dv in (1, 3):
            side = 0 if dv == 1 else 1
            landed(vq.at[h, du, side], vq_r.at[h, du, side])
            add(h, k, side, [vq.at[h, du, side]])
            hand(h, k, None, at(*offset(h, 0, dv)), vf.at[h, du, side], vf_r.at[h, du, side])
            return
        for side in (0, 1):
            landed(vf.at[h, du, side], vf_r.at[h, du, side])
        if du == 0:
            for side in (0, 1):
                landed(uf.at[h, side], uf_r.at[h, side])

            def last(i, carry):
                here = pl.ds(pl.multiple_of(h * half + i * 16, 16), 16)
                there = pl.ds(pl.multiple_of(i * 16, 16), 16)
                total = acc[here, :] + xbuf[k, here, :].astype(jnp.float32)
                for side in (0, 1):
                    total = total + vf[h, du, side, there, :].astype(jnp.float32)
                    total = total + uf[h, side, there, :].astype(jnp.float32)
                acc[here, :] = total
                return carry

            lax.fori_loop(0, half // 16, last, 0)
            return
        add(h, k, None, [vf.at[h, du, 0], vf.at[h, du, 1]])
        if du == 2:
            hand(h, k, 0, at(*offset(h, 1, 0)), uq.at[h, 0], uq_r.at[h, 0])
            hand(h, k, 1, at(*offset(h, 3, 0)), uq.at[h, 1], uq_r.at[h, 1])
            return
        side = 0 if du == 1 else 1
        landed(uq.at[h, side], uq_r.at[h, side])
        add(h, k, side, [uq.at[h, side]])
        hand(h, k, None, at(*offset(h, du, 0)), uf.at[h, side], uf_r.at[h, side])

    for group, early, late in BACK:
        backward(group)
        for step_of in early:
            relay(*step_of)
        gather(group)
        for step_of in late:
            relay(*step_of)

    def gate_gradient(s, carry):
        gg = jnp.sum(actr[s] * nref[s], axis=1, keepdims=True)
        ggsend[s] = jnp.sum(
            jnp.where(slot == rk[s * 2 + core], gg, 0.0), axis=0, keepdims=True
        )
        return carry

    lax.fori_loop(0, WAYS, gate_gradient, 0)
    to_all(lambda e: ggsend.at[e], gown, 4)
    gown[me] = ggsend[me]
    backward(((0, 0),))
    gather(((0, 0),))

    from_all(zbuf, 3, planes - 1)
    eye_r = lax.broadcasted_iota(jnp.int32, (planes, planes), 0)
    eye_c = lax.broadcasted_iota(jnp.int32, (planes, planes), 1)
    eye = eye_r == eye_c

    def column(row):
        return jnp.sum(jnp.where(eye, row, 0.0), axis=1, keepdims=True)

    g_row = grades[...].astype(jnp.float32)
    g_col = column(g_row)
    s_col = zbuf[:, 0, 0:1]
    s_row = jnp.sum(jnp.where(eye, s_col, 0.0), axis=0, keepdims=True)
    ln2 = 0.6931471805599453
    d_row = ln2 / jnp.log(2.0 + ranks[...].astype(jnp.float32))
    d_col = column(d_row)
    worth_row = jnp.exp2(g_row)
    worth_col = column(worth_row)
    ahead = jnp.logical_or(g_row > g_col, jnp.logical_and(g_row == g_col, eye_c < eye_r))
    ideal = jnp.sum(jnp.where(ahead, 1.0, 0.0), axis=1, keepdims=True)
    ideal_gain = jnp.sum((worth_col - 1.0) * ln2 / jnp.log(2.0 + ideal), axis=0, keepdims=True)
    swap = jnp.abs((worth_col - worth_row) * (d_col - d_row)) / ideal_gain
    swap = jnp.where(g_col > g_row, swap, 0.0)
    margin = s_col - s_row
    soft = jnp.maximum(-margin, 0.0) + jnp.log(1.0 + jnp.exp(-jnp.abs(margin)))
    loss = total(swap * soft)
    pull = swap / (1.0 + jnp.exp(margin))
    d_own = jnp.sum(jnp.where(eye_c == z, pull, 0.0) - jnp.where(eye_r == z, pull, 0.0))
    spot_of = lax.broadcasted_iota(jnp.int32, stat_o.shape, 1)
    stat_o[...] = jnp.where(spot_of == 0, loss, score)
    scale = d_own * (LOSS_SCALE / tokens)

    from_all(gown, 4)
    gate_grad = gown[:, 0, :]
    gates = gate_s[...]
    d_logit = gates * (gate_grad - jnp.sum(gates * gate_grad, axis=0, keepdims=True))
    d_logit = split3(d_logit)
    rout3 = jnp.concatenate([rout_t[...]] * 3, axis=0)
    acc[...] = dot(d_logit, rout3, TN)
    head = headrow[...]

    def finish(i, carry):
        rows = pl.ds(pl.multiple_of(i * 16, 16), 16)
        h = hid[rows, :].astype(jnp.float32)
        r = rinv[rows, :]
        scaled = acc[rows, :] * gain[...]
        lean = jnp.mean(h * scaled, axis=1, keepdims=True)
        full = r * scaled - h * (r * r * r * lean) + head
        out_o[rows, :] = (full * scale).astype(jnp.bfloat16)
        return carry

    for h in (0, 1):
        relay(h, 0, 0)
        lax.fori_loop(h * half // 16, (h + 1) * half // 16, finish, 0)
    for copy in back + hops:
        copy.wait_send()
    sent_all(grecv, 0, 2 * (WAYS - 1))
    sent_all(tsend, 1)
    sent_all(hbuf, 2)
    sent_all(zbuf, 3, planes - 1)
    sent_all(gown, 4)


def local(
    hidden,
    norm_gain,
    router,
    gate_proj,
    up_proj,
    down_proj,
    final_gain,
    score_vector,
    expert_ids,
    grades,
    passage_ranks,
):
    tokens, width = hidden.shape[2:]
    units = gate_proj.shape[2]
    planes = lax.axis_size("psg")
    f32, bf16 = jnp.float32, jnp.bfloat16
    vmem = pl.BlockSpec(memory_space=pltpu.VMEM)
    any_space = pl.BlockSpec(memory_space=pl.ANY)
    scratch = [
        pltpu.VMEM((WAYS, tokens, width), bf16),
        pltpu.VMEM((width, units), bf16),
        pltpu.VMEM((width, units), bf16),
        pltpu.VMEM((units, width), bf16),
        pltpu.VMEM((WAYS, tokens), f32),
        pltpu.VMEM((tokens, 1), f32),
        pltpu.VMEM((1, width), f32),
        pltpu.VMEM((WAYS, 1, tokens), f32),
        pltpu.VMEM((2 * WAYS, 1, tokens), f32),
        pltpu.VMEM((2 * WAYS, 1, tokens), f32),
        pltpu.VMEM((8 * SLOTS, max(width, 2 * units)), bf16),
        pltpu.VMEM((WAYS, SLOTS, units), f32),
        pltpu.VMEM((WAYS, SLOTS, units), f32),
        pltpu.VMEM((WAYS, SLOTS, units), f32),
        pltpu.VMEM((WAYS, 1, units), f32),
        pltpu.VMEM((WAYS, width // 128, 128), f32),
        pltpu.VMEM((WAYS, width // 128, 128), bf16),
        pltpu.VMEM((WAYS, width // 128, 128), bf16),
        pltpu.VMEM((WAYS, width // 128, 128), bf16),
        pltpu.VMEM((1, width), f32),
        pltpu.VMEM((WAYS, width), bf16),
        pltpu.VMEM((WAYS, 1, units), f32),
        pltpu.VMEM((planes, 1, tokens), f32),
        pltpu.VMEM((16, SLOTS, width), bf16),
        pltpu.VMEM((16, SLOTS, width), bf16),
        pltpu.VMEM((2, 4, 2, tokens // 4, width), bf16),
        pltpu.VMEM((2, 4, 2, tokens // 2, width), bf16),
        pltpu.VMEM((2, 2, tokens // 4, width), bf16),
        pltpu.VMEM((2, 2, tokens // 2, width), bf16),
        pltpu.VMEM((WAYS, 1, tokens), f32),
        pltpu.VMEM((WAYS, 1, tokens), f32),
        pltpu.VMEM((tokens, width), f32),
        pltpu.SemaphoreType.DMA((3,)),
        pltpu.SemaphoreType.DMA((44,)),
        pltpu.SemaphoreType.DMA((2, 16, 2)),
        pltpu.SemaphoreType.DMA((2, 16)),
        pltpu.SemaphoreType.DMA((2, 16)),
        pltpu.SemaphoreType.DMA((5,)),
        pltpu.SemaphoreType.DMA((5,)),
        pltpu.SemaphoreType.DMA((2, 16)),
        pltpu.SemaphoreType.DMA((2, 16)),
        pltpu.SemaphoreType.DMA((40,)),
        pltpu.SemaphoreType.DMA((2, 4, 2)),
        pltpu.SemaphoreType.DMA((2, 4, 2)),
        pltpu.SemaphoreType.DMA((2, 2)),
        pltpu.SemaphoreType.DMA((2, 2)),
        pltpu.SemaphoreType.REGULAR((4,)),
    ]
    stat, grad = pl.pallas_call(
        kernel,
        out_shape=(
            jax.ShapeDtypeStruct((1, 128), f32),
            jax.ShapeDtypeStruct((tokens, width), bf16),
        ),
        in_specs=[vmem] * 8 + [any_space] * 3,
        out_specs=(vmem, vmem),
        scratch_shapes=scratch,
        compiler_params=pltpu.CompilerParams(
            collective_id=0, has_side_effects=True, vmem_limit_bytes=62 * 1024 * 1024
        ),
        name="expert_block",
    )(
        hidden.reshape(tokens, width),
        expert_ids.reshape(tokens, -1).T,
        norm_gain.reshape(1, width),
        router.T,
        final_gain.reshape(width // 128, 128),
        score_vector.reshape(width // 128, 128),
        grades,
        passage_ranks,
        gate_proj[0],
        up_proj[0],
        down_proj[0],
    )
    return stat[0, 0:1], stat[0:1, 1:2], grad.reshape(1, 1, tokens, width)


def solution(mesh):
    placed = (
        P("exp", "psg", None, None),
        P(),
        P(),
        P("exp", None, None),
        P("exp", None, None),
        P("exp", None, None),
        P(),
        P(),
        P("exp", "psg", None, None),
        P("exp", None),
        P("exp", None),
    )
    return jax.shard_map(
        local,
        mesh=mesh,
        in_specs=placed,
        out_specs=(P("exp"), P("exp", "psg"), P("exp", "psg", None, None)),
        check_vma=False,
    )
```
